32 devices in a mesh: wide: 16 (over z, y, core), narrow: 2 (over x).
Axes of the slice: x: 2, y: 2, z: 4, core: 2. Of those that a mesh axis runs over, the one named last changes fastest.
Arguments:
- valence: float32 [8, 32768], P(None, ('wide', 'narrow')), may hold values from -6 to 6
- conduction: float32 [32, 32768], P(('wide', 'narrow')), may hold values from -6 to 6
- eps_val: float32 [8], replicated, may hold values from -12 to -2
- eps_cond: float32 [32], replicated, may hold values from 0.5 to 20
- omega: float32 [6], replicated, may hold values from 0.3 to 30
- gmap: int32 [8192], replicated, may hold values from 0 to 32767, as said below
Outputs:
- chi: float32 [6, 8192, 8192], P(None, 'wide', 'narrow')
The draws below stay inside these ranges and needn't reach their ends.
Inputs may be any that keep to these rules, and one draw needn't show every extreme that they name: `gmap`: distinct grid indices: the 8192 grid points of smallest squared wave vector (frequencies folded to -16 .. 15), equal lengths in random order, listed by rising length.
All inputs are finite; a program needn't handle non-finite values.
Results may differ from the reference program's by a relative error of at most 0.0042.
Values may be sent and summed in bfloat16 or wider, within the bound.
A program may use at most 128 MiB of HBM per device.

```python
import math
import jax
import jax.numpy as jnp
from jax import lax

GRID = 32
NPW = 8192
NV = 8
NW = 6
NGRID = 32768
NC = 32
NPAIR = 256


def draw_gmap(key, part):
    flat_index = jnp.arange(GRID * GRID * GRID, dtype=jnp.int32)
    coord_x = flat_index // (GRID * GRID)
    coord_y = flat_index // GRID % GRID
    coord_z = flat_index % GRID
    fold_x = jnp.where(coord_x < GRID // 2, coord_x, coord_x - GRID)
    fold_y = jnp.where(coord_y < GRID // 2, coord_y, coord_y - GRID)
    fold_z = jnp.where(coord_z < GRID // 2, coord_z, coord_z - GRID)
    length_sq = fold_x * fold_x + fold_y * fold_y + fold_z * fold_z
    tiebreak = jax.random.permutation(jax.random.fold_in(key, 17), GRID * GRID * GRID).astype(jnp.int32)
    scores = length_sq * (GRID * GRID * GRID) + tiebreak
    ordered = jnp.argsort(scores, stable=True)
    return ordered[:NPW].astype(jnp.int32)


def block_scale(stream_key, dims, split, low, high):
    level, own = 1.0, jax.random.fold_in(stream_key, 6)
    for position, parts in split:
        draws = jnp.exp(jax.random.uniform(jax.random.fold_in(own, position), (parts,), jnp.float32, low / len(split), high / len(split)))
        level = level * jnp.repeat(draws, dims[position] // parts).reshape([-1 if axis == position else 1 for axis in range(len(dims))])
    return level


def centred(stream_key, shape, width, limit, cuts=(), kind=jnp.bfloat16):
    result = jax.random.normal(stream_key, shape, jnp.float32) * width
    if len(cuts) > 0:
        result = block_scale(stream_key, shape, cuts, -0.22, 0.18) * result
    return jnp.clip(result, min=-limit, max=limit).astype(kind)


def setup_inputs(seed: int = 0) -> dict:
    key_of = jax.random.split(jax.random.key(seed), 7)
    valence = centred(key_of[0], (NV, NGRID), 1.0, 6.0, ((1, 32),), jnp.float32)
    conduction = centred(key_of[1], (NC, NGRID), 1.0, 6.0, ((0, 32),), jnp.float32)
    eps_val = jnp.clip(jax.random.uniform(key_of[2], (NV,), jnp.float32, -12.0, -2.0), -12.0, -2.0)
    eps_cond = jnp.clip(jax.random.uniform(key_of[3], (NC,), jnp.float32, 0.5, 20.0), 0.5, 20.0)
    omega = jnp.clip(jnp.exp(jax.random.uniform(key_of[4], (NW,), jnp.float32, math.log(0.3), math.log(30.0))), 0.3, 30.0)
    gmap = draw_gmap(jax.random.fold_in(key_of[6], 71), 0)
    return dict(valence=valence, conduction=conduction, eps_val=eps_val, eps_cond=eps_cond, omega=omega, gmap=gmap)


def reference(valence, conduction, eps_val, eps_cond, omega, gmap):
    cube = valence.reshape(NV, GRID, GRID, GRID)
    norm_factor = 1.0 / jnp.sqrt(jnp.float32(NGRID))

    def one_band(band):
        product = cube * band.reshape(1, GRID, GRID, GRID)
        spectrum = jnp.fft.fftn(product, axes=(1, 2, 3)).reshape(NV, NGRID)
        picked = spectrum[:, gmap] * norm_factor
        return jnp.stack([jnp.real(picked), jnp.imag(picked)]).astype(jnp.bfloat16)
    stacked = lax.map(one_band, conduction)
    pairs = jnp.transpose(stacked, (1, 0, 2, 3)).reshape(2, NPAIR, NPW)
    energy_gap = (eps_cond[:, None] - eps_val[None, :]).reshape(NPAIR)
    weights = -2.0 * energy_gap[None, :] / (energy_gap[None, :] ** 2 + omega[:, None] ** 2)
    weights = weights / jnp.sqrt(jnp.float32(NPAIR))
    pair_float = pairs.astype(jnp.float32).reshape(2 * NPAIR, NPW)

    def one_freq(row_weight):
        scaled = (pairs.astype(jnp.float32) * row_weight[None, :, None]).astype(jnp.bfloat16)
        scaled = lax.optimization_barrier(scaled).astype(jnp.float32).reshape(2 * NPAIR, NPW)
        return jnp.dot(scaled.T, pair_float, preferred_element_type=jnp.float32, precision=lax.Precision.HIGHEST)
    return lax.map(one_freq, weights)
```

```python
import functools
import math

import jax
import jax.numpy as jnp
import numpy as np
from jax import lax
from jax.experimental import pallas as pl
from jax.experimental.pallas import tpu as pltpu
from jax.sharding import PartitionSpec as P

GRID = 32
MESH = pl.DeviceIdType.MESH
VMEM = pltpu.MemorySpace.VMEM
HBM = pltpu.MemorySpace.HBM
SMEM = pltpu.MemorySpace.SMEM


def wide_factors(wide):
    chips = wide // 2
    inner = 2 ** (int(math.log2(chips)) // 2)
    return chips // inner, inner


@functools.lru_cache(None)
def tables(num_waves, num_val):
    fold = np.arange(GRID)
    fold = np.where(fold < GRID // 2, fold, fold - GRID)
    squares = fold**2
    lengths = (squares[:, None, None] + squares[None, :, None] + squares[None, None, :]).reshape(-1)
    limit = int(np.sort(lengths)[num_waves - 1])
    reach = math.isqrt(limit)
    assert reach < GRID // 2
    half = [
        (ky, kz)
        for ky in range(-reach, reach + 1)
        for kz in range(0, reach + 1)
        if ky * ky + kz * kz <= limit and (kz > 0 or ky >= 0)
    ]
    count = -(-len(half) // 128) * 128
    kys = np.array([k for k, _ in half])
    kzs = np.array([k for _, k in half])
    points = np.arange(GRID)
    turn = 2.0 * np.pi / GRID
    phase = (points[:, None, None] * kys + points[None, :, None] * kzs) % GRID
    phase = phase.reshape(GRID * GRID, len(half)) * turn
    plane = np.zeros((GRID * GRID, 2 * count))
    plane[:, : len(half)] = np.cos(phase)
    plane[:, count : count + len(half)] = -np.sin(phase)
    codes = np.full((count, 2), -1, np.int32)
    codes[: len(half), 0] = (kys % GRID) * GRID + kzs % GRID
    codes[: len(half), 1] = (-kys % GRID) * GRID + -kzs % GRID
    kxs = np.arange(-reach, reach + 1)
    line = (kxs[:, None] * points[None, :] % GRID) * turn
    eye = np.eye(num_val)
    norm = 1.0 / math.sqrt(GRID**3)
    cosine = np.kron(np.cos(line), eye) * norm
    sine = np.kron(np.sin(line), eye) * norm
    return plane, codes, np.stack([cosine, sine]), reach


def round_up(count, step):
    return -(-count // step) * step


@functools.lru_cache(None)
def half_lists(num_waves, narrow, tiles):
    fold = np.arange(GRID)
    fold = np.where(fold < GRID // 2, fold, fold - GRID)
    kx, ky, kz = [k.reshape(-1) for k in np.meshgrid(fold, fold, fold, indexing="ij")]
    lengths = kx * kx + ky * ky + kz * kz
    ordered = np.sort(lengths)[:num_waves]
    half = (kz > 0) | ((kz == 0) & ((ky > 0) | ((ky == 0) & (kx >= 0))))
    chosen = np.nonzero(half & (lengths <= ordered[-1]))[0]
    chosen = chosen[np.argsort(lengths[chosen], kind="stable")]
    sizes = lengths[chosen]
    part = num_waves // narrow
    ends = []
    for n in range(narrow):
        begin = np.searchsorted(sizes, ordered[n * part])
        ends.append((begin, np.searchsorted(sizes, ordered[(n + 1) * part - 1], side="right")))
    below, above = 0, {tile: 0 for tile in tiles}
    for n, (begin, _) in enumerate(ends):
        for tile in tiles:
            for t in range(part // tile):
                g = n * part + t * tile
                low = np.searchsorted(sizes, ordered[g]) - begin - t * tile // 2
                high = np.searchsorted(sizes, ordered[g + tile - 1], side="right") - begin - t * tile // 2
                below, above[tile] = max(below, -int(low)), max(above[tile], int(high))
    windows = {tile: round_up(below + above[tile], 128) for tile in tiles}
    slots = max((part // tile - 1) * tile // 2 + windows[tile] for tile in tiles)
    slots = max(slots, round_up(below + max(end - begin for begin, end in ends), 128))
    lists = np.full((narrow, 1, slots), -1, np.int32)
    for n, (begin, end) in enumerate(ends):
        lists[n, 0, below : below + end - begin] = chosen[begin:end]
    return lists, windows


def np_halves(table):
    table = np.asarray(table, np.float32)
    high = table.astype(jnp.bfloat16)
    return high, (table - high.astype(np.float32)).astype(jnp.bfloat16)


def split_bf16(x):
    high = x.astype(jnp.bfloat16)
    return high, (x - high.astype(jnp.float32)).astype(jnp.bfloat16)


def dot(a, b):
    return jnp.dot(a, b, preferred_element_type=jnp.float32)


def dot3(a, b_high, b_low):
    a_high, a_low = split_bf16(a)
    return dot(a_high, b_high) + (dot(a_low, b_high) + dot(a_high, b_low))


def dot3_left(a_high, a_low, b):
    b_high, b_low = split_bf16(b)
    return dot(a_high, b_high) + (dot(a_high, b_low) + dot(a_low, b_high))


def flip(i, mask, size):
    assert size & (size - 1) == 0
    out, bit = i, 1
    while bit < size:
        if mask & bit:
            out = out + bit * (1 - 2 * lax.rem(i // bit, 2))
        bit *= 2
    return out


class Place:
    def __init__(self, wide, narrow):
        self.outer, self.inner = wide_factors(wide)
        self.wide, self.narrow = wide, narrow
        self.w, self.n = lax.axis_index("wide"), lax.axis_index("narrow")
        self.core = lax.rem(self.w, 2)
        self.y = lax.rem(self.w // 2, self.inner)
        self.z = self.w // (2 * self.inner)
        self.sizes = dict(z=self.outer, y=self.inner, x=narrow)

    def wide_at(self, zz, yy, cc):
        return (zz * self.inner + yy) * 2 + cc

    def slot(self, zz, yy, cc, nn):
        return self.wide_at(zz, yy, cc) * self.narrow + nn

    def moved(self, masks):
        return (
            flip(self.z, masks.get("z", 0), self.outer),
            flip(self.y, masks.get("y", 0), self.inner),
            flip(self.n, masks.get("x", 0), self.narrow),
        )

    def device(self, masks):
        zz, yy, nn = self.moved(masks)
        return (self.wide_at(zz, yy, self.core), nn)

    def peers(self):
        found = []
        for dim, size in self.sizes.items():
            found += [self.device({dim: m}) for m in range(1, size)]
        other = self.wide_at(self.z, self.y, 1 - self.core)
        found += [(other, flip(self.n, m, self.narrow)) for m in range(self.narrow)]
        return found


def count_first(sizes, order):
    a, b, c = [sizes[dim] for dim in order]
    return (a - 1 + b - 1 + c - 1 + 1) + (a - 1) * (b - 1 + c - 1 + 1) + (b - 1) * a * (c - 1 + 1) + (c - 1) * a * b


ORDERS = (("z", "y", "x"), ("z", "x", "y"))


def first_gather(place, order, src, view, send_sem, recv_sem):
    sizes = [place.sizes[dim] for dim in order]
    partner = (place.wide_at(place.z, place.y, 1 - place.core), place.n)
    count = [0]

    def send(ref, index, target):
        pltpu.make_async_remote_copy(
            src_ref=ref,
            dst_ref=view(index),
            send_sem=send_sem.at[count[0]],
            recv_sem=recv_sem.at[index],
            device_id=target,
            device_id_type=MESH,
        ).start()
        count[0] += 1

    def arrived(index):
        pltpu.make_async_remote_copy(
            src_ref=view(index),
            dst_ref=view(index),
            send_sem=send_sem.at[0],
            recv_sem=recv_sem.at[index],
            device_id=partner,
            device_id_type=MESH,
        ).wait_recv()

    def index_of(masks):
        zz, yy, nn = place.moved(masks)
        return place.slot(zz, yy, place.core, nn)

    mine = index_of({})
    for dim, size in zip(order, sizes):
        for m in range(size - 1, 0, -1):
            send(src, mine, place.device({dim: m}))
    send(src, mine, partner)
    for level in range(3):
        lower = [{}]
        for dim, size in zip(order[:level], sizes[:level]):
            lower = [{**masks, dim: m} for masks in lower for m in range(size)]
        for m in range(1, sizes[level]):
            for masks in lower:
                index = index_of({**masks, order[level]: m})
                arrived(index)
                for dim, size in zip(order[level + 1 :], sizes[level + 1 :]):
                    for k in range(size - 1, 0, -1):
                        send(view(index), index, place.device({dim: k}))
                send(view(index), index, partner)
    assert count[0] == count_first(place.sizes, order)


def pairs_kernel(wide, narrow, reach, slots, row_window, row_step, *refs):
    src, sources = refs[0], refs[1:8]
    cols, rows = refs[8:10]
    val, held = refs[10], refs[11:18]
    stage, picked, pick_hot, pick_x, pick_sign, local = refs[18:24]
    first_send, first_recv, own_sem, load_sem, send_sem, recv_sem, row_recv = refs[24:31]
    cond, plane_h, plane_l, line_h, line_l, codes, wanted = held
    place = Place(wide, narrow)
    core, n, w, z, y = place.core, place.n, place.w, place.z, place.y
    outer, inner = place.outer, place.inner
    grid, num_val, plane = val.shape
    chunk = src.shape[1]
    per = plane // chunk
    count = codes.shape[0]
    kinds = 2 * reach + 1
    size = kinds * num_val

    copies = [pltpu.make_async_copy(a, b, load_sem.at[i]) for i, (a, b) in enumerate(zip(sources, held))]
    for i in (5, 6, 0, 1, 2, 3, 4):
        copies[i].start()

    peers = place.peers()
    barrier = pltpu.get_barrier_semaphore()
    for peer in peers:
        pl.semaphore_signal(barrier, inc=1, device_id=peer, device_id_type=MESH)
    pl.semaphore_wait(barrier, len(peers))

    def view(index):
        if per == 1:
            return val.at[index]
        return val.at[index // per, :, pl.ds(pl.multiple_of(lax.rem(index, per) * chunk, chunk), chunk)]

    mine = place.slot(z, y, core, n)
    own = pltpu.make_async_copy(src, view(mine), own_sem)
    own.start()

    def prepare():
        copies[5].wait()
        copies[6].wait()
        first, second = codes[:, 0:1], codes[:, 1:2]
        tile = 256 if pick_hot.shape[1] % 256 == 0 else 128

        def body(t, carry):
            here = pl.ds(pl.multiple_of(t * tile, tile), tile)
            index = wanted[:, here]
            kx = index // (GRID * GRID)
            code = index % (GRID * GRID)
            ky, kz = code // GRID, code % GRID
            kx = jnp.where(kx < GRID // 2, kx, kx - GRID)
            direct = ((kz > 0) & (kz < GRID // 2)) | ((kz == 0) & (ky < GRID // 2))
            pick_x[:, here] = jnp.where(direct, kx, -kx) + reach
            pick_sign[:, here] = jnp.where(direct, 1.0, -1.0).astype(jnp.float32)
            hit = (code == first) | (code == second)
            pick_hot[:, here] = jnp.where(hit, 1.0, 0.0).astype(jnp.bfloat16)
            return carry

        lax.fori_loop(0, pick_hot.shape[1] // tile, body, 0)

    for side in range(2):
        @pl.when(core == side)
        def _():
            first_gather(place, ORDERS[side], src, view, first_send, first_recv)

    own.wait()
    prepare()
    step = narrow // per

    def flat(cc):
        copies_of = [(2 * q + cc) * step for q in range(wide // 2)]
        field = [(val[pl.ds(p, step)] * cond[pl.ds(p, step)]).reshape(step * num_val, plane) for p in copies_of]
        result = dot3(jnp.concatenate(field, axis=0), plane_h[...], plane_l[...])
        for q, p in enumerate(copies_of):
            part = result[q * step * num_val : (q + 1) * step * num_val]
            stage[pl.ds(p, step)] = part.reshape(step, num_val, 2 * count)

    for i in range(3):
        copies[i].wait()
    flat(core)
    for zz in range(outer):
        for yy in range(inner):
            for nn in range(narrow):
                index = place.slot(zz, yy, 1 - core, nn)
                pltpu.make_async_copy(view(index), view(index), first_recv.at[index]).wait()
    flat(1 - core)
    copies[3].wait()
    copies[4].wait()
    whole = stage[...].reshape(grid * num_val, 2 * count)
    real, imag = whole[:, :count], whole[:, count:]
    cos_h, sin_h, cos_l, sin_l = line_h[0], line_h[1], line_l[0], line_l[1]
    picked[:size, :] = (dot3_left(cos_h, cos_l, real) + dot3_left(sin_h, sin_l, imag)).astype(jnp.bfloat16)
    picked[size:, :] = (dot3_left(cos_h, cos_l, imag) - dot3_left(sin_h, sin_l, real)).astype(jnp.bfloat16)

    def pick(half, store):
        base = pl.multiple_of(half * slots, 128)
        for begin in range(0, slots, 512):
            tile = min(512, slots - begin)
            here = pl.ds(pl.multiple_of(base + begin, 128), tile)
            columns = dot(picked[...], pick_hot[:, here]).reshape(2, kinds, num_val, tile)
            kx = jnp.broadcast_to(pick_x[:, here], (num_val, tile))
            sign = pick_sign[:, here]
            real = jnp.zeros((num_val, tile), jnp.float32)
            imag = jnp.zeros((num_val, tile), jnp.float32)
            for k in range(kinds):
                keep = kx == k
                real = jnp.where(keep, columns[0, k], real)
                imag = jnp.where(keep, columns[1, k], imag)
            store(begin, tile, jnp.concatenate([real, imag * sign], axis=0).astype(jnp.bfloat16))

    partner = (place.wide_at(z, y, 1 - core), n)
    pending = []

    def send(src_ref, dst_ref, target, sem, when=None):
        k = len(pending)
        pltpu.make_async_remote_copy(
            src_ref=src_ref,
            dst_ref=dst_ref,
            send_sem=send_sem.at[k],
            recv_sem=sem,
            device_id=target,
            device_id_type=MESH,
        ).start()
        pending.append((when, src_ref.shape))

    def forward(index, target, when=None):
        send(cols.at[index], cols.at[index], target, recv_sem.at[index], when)

    def arrived(index):
        pltpu.make_async_copy(cols.at[index], cols.at[index], recv_sem.at[index]).wait()

    holder = w // (wide // narrow)
    window_of = lambda ww: pl.multiple_of(lax.rem(ww, wide // narrow) * row_step, 128)
    others = [m for m in range(1, narrow)]

    def row_sends(zz, yy, when):
        start = place.slot(zz, yy, core, 0)
        group = (zz * inner + yy) * 2 + core

        @pl.when(n == holder)
        def _():
            for cc in (core, 1 - core):
                ww = place.wide_at(z, y, cc)
                for m in others:
                    send(
                        cols.at[pl.ds(start, narrow), :, pl.ds(window_of(ww), row_window)],
                        rows.at[pl.ds(start, narrow)],
                        (ww, flip(n, m, narrow)),
                        row_recv.at[group],
                        (when, "row"),
                    )

    for m in range(narrow - 1, 0, -1):
        half = flip(n, m, narrow)

        def store(begin, tile, value, m=m):
            local[m - 1, :, begin : begin + tile] = value

        pick(half, store)
        send(local.at[m - 1], cols.at[mine], (w, half), recv_sem.at[mine])

    def store_own(begin, tile, value):
        cols[mine, :, begin : begin + tile] = value

    pick(n, store_own)
    right, left = (place.wide_at(z + 1, y, core), n), (place.wide_at(z - 1, y, core), n)

    def spread(index, when, go_right, go_left):
        if go_right:
            @pl.when(z < outer - 1)
            def _():
                forward(index, right, (when, "right"))
        if go_left:
            @pl.when(z > 0)
            def _():
                forward(index, left, (when, "left"))
        for m in range(1, inner):
            forward(index, place.device({"y": m}), (when, None))
        forward(index, partner, (when, None))

    spread(mine, None, True, True)
    for m in others:
        index = place.slot(z, y, core, flip(n, m, narrow))
        arrived(index)
        spread(index, None, True, True)
    row_sends(z, y, None)

    def side_blocks(zz, when):
        for m in range(1, inner):
            yy = flip(y, m, inner)
            for k in range(narrow):
                index = place.slot(zz, yy, core, flip(n, k, narrow))
                arrived(index)
                forward(index, partner, (when, None))
            row_sends(zz, yy, when)

    def present(offset):
        return (z + offset >= 0) & (z + offset < outer)

    for s in range(1, outer):
        for offset in (-s, s):
            @pl.when(present(offset))
            def _():
                for k in range(narrow):
                    index = place.slot(z + offset, y, core, flip(n, k, narrow))
                    arrived(index)
                    spread(index, offset, offset < 0, offset > 0)
                row_sends(z + offset, y, offset)
        if s == 1:
            side_blocks(z, None)
        else:
            for offset in (1 - s, s - 1):
                @pl.when(present(offset))
                def _():
                    side_blocks(z + offset, offset)
    for offset in (1 - outer, outer - 1) if outer > 1 else ():
        @pl.when(present(offset))
        def _():
            side_blocks(z + offset, offset)
    if outer == 1:
        side_blocks(z, None)

    for zz in range(outer):
        for yy in range(inner):
            for nn in range(narrow):
                arrived(place.slot(zz, yy, 1 - core, nn))

    @pl.when(n == holder)
    def _():
        rows[...] = cols[:, :, pl.ds(window_of(w), row_window)]

    @pl.when(n != holder)
    def _():
        for group in range(wide):
            rows_of = rows.at[pl.ds(group * narrow, narrow)]
            pltpu.make_async_copy(rows_of, rows_of, row_recv.at[group]).wait()

    def drain(k, shape):
        ref = cols.at[0] if len(shape) == 2 else rows.at[pl.ds(0, narrow)]
        pltpu.make_async_copy(ref, ref, send_sem.at[k]).wait()

    waits = {}
    for k, (when, shape) in enumerate(pending):
        when = when if isinstance(when, tuple) else (when, None)
        waits.setdefault(when, []).append((k, shape))
    for (offset, kind), items in waits.items():
        test = None
        if offset is not None:
            test = present(offset)
        extra = {"right": z < outer - 1, "left": z > 0, "row": n == holder}.get(kind)
        if extra is not None:
            test = extra if test is None else test & extra

        def all_of(items=items):
            for k, shape in items:
                drain(k, shape)

        if test is None:
            all_of()
        else:
            pl.when(test)(all_of)

    for side, order in enumerate(ORDERS):
        @pl.when(core == side)
        def _():
            for k in range(count_first(place.sizes, order)):
                pltpu.make_async_copy(src, src, first_send.at[k]).wait()


def second_sends(outer, inner, narrow):
    spread = 2 + (inner - 1) + 1
    row = 2 * (narrow - 1)
    sides = (inner - 1) * (narrow + row)
    total = narrow - 1 + narrow * spread + row + sides
    return total + 2 * (outer - 1) * (narrow * (spread - 1) + row + sides)


def gather_pairs(val, cond, num_waves, lists, row_window, row_step, wide, narrow):
    num_val, chunk = val.shape
    table, codes, line, reach = tables(num_waves, num_val)
    plane_h, plane_l = np_halves(table)
    line_h, line_l = np_halves(line)
    slots = lists.shape[2]
    wanted = np.maximum(lists.reshape(1, -1), 0)
    outer, inner = wide_factors(wide)
    devices = wide * narrow
    count = codes.shape[0]
    plane = GRID * GRID
    kinds = 2 * reach + 1
    operands = (cond, plane_h, plane_l, line_h, line_l, codes, wanted)
    held = [pltpu.VMEM(x.shape, x.dtype) for x in operands]
    sizes = dict(z=outer, y=inner, x=narrow)
    sends = max(count_first(sizes, order) for order in ORDERS)
    depth = 2 * num_val
    return pl.pallas_call(
        functools.partial(pairs_kernel, wide, narrow, reach, slots, row_window, row_step),
        out_shape=[
            jax.ShapeDtypeStruct((devices, depth, slots), jnp.bfloat16),
            jax.ShapeDtypeStruct((devices, depth, row_window), jnp.bfloat16),
        ],
        in_specs=[pl.BlockSpec(memory_space=pl.ANY)] * 8,
        out_specs=[pl.BlockSpec(memory_space=VMEM)] * 2,
        scratch_shapes=[pltpu.VMEM((GRID, num_val, plane), jnp.float32)]
        + held
        + [
            pltpu.VMEM((GRID, num_val, 2 * count), jnp.float32),
            pltpu.VMEM((2 * kinds * num_val, count), jnp.bfloat16),
            pltpu.VMEM((count, narrow * slots), jnp.bfloat16),
            pltpu.VMEM((1, narrow * slots), jnp.int32),
            pltpu.VMEM((1, narrow * slots), jnp.float32),
            pltpu.VMEM((narrow - 1, depth, slots), jnp.bfloat16),
            pltpu.SemaphoreType.DMA((sends,)),
            pltpu.SemaphoreType.DMA((devices,)),
            pltpu.SemaphoreType.DMA,
            pltpu.SemaphoreType.DMA((7,)),
            pltpu.SemaphoreType.DMA((second_sends(outer, inner, narrow),)),
            pltpu.SemaphoreType.DMA((devices,)),
            pltpu.SemaphoreType.DMA((wide,)),
        ],
        compiler_params=pltpu.CompilerParams(
            collective_id=0, has_side_effects=True, vmem_limit_bytes=48 << 20
        ),
    )(val, *[jnp.asarray(x) for x in operands])


def expand(held, listed, index, num_val):
    depth, slots = held.shape
    tile = index.shape[1]
    area = GRID * GRID
    lx, ly, lz = listed // area, listed // GRID % GRID, listed % GRID
    mirror = (GRID - lx) % GRID * area + (GRID - ly) % GRID * GRID + (GRID - lz) % GRID
    mirror = jnp.where(listed < 0, -1, mirror)

    def column(row):
        turned = jnp.broadcast_to(row, (128, slots)).T
        return jnp.concatenate([turned] * (tile // 128), axis=1)

    hit = (index == column(listed)) | (index == column(mirror))
    values = dot(held, jnp.where(hit, 1.0, 0.0).astype(jnp.bfloat16))
    kx, ky, kz = index // area, index // GRID % GRID, index % GRID
    low = GRID // 2
    direct = ((kz > 0) & (kz < low)) | (
        (kz == 0) & (((ky > 0) & (ky < low)) | ((ky == 0) & (kx < low)))
    )
    sign = jnp.where(direct, 1.0, -1.0).astype(jnp.float32)
    row = lax.broadcasted_iota(jnp.int32, (depth, tile), 0)
    return values * jnp.where(row // num_val % 2 == 1, sign, 1.0)


def chi_kernel(num_cond, num_val, window, scalars, gmap, lists, rows, columns, out, scaled):
    num, row_width, tile = out.shape
    depth = rows.shape[0]
    narrow, wide = lists.shape[0], gmap.shape[1] // row_width
    w, n = lax.axis_index("wide"), lax.axis_index("narrow")
    step = pl.program_id(0)

    @pl.when(step == 0)
    def _():
        lane = lax.broadcasted_iota(jnp.int32, (1, depth), 1)
        band, orbital = lane // (2 * num_val), lane % num_val

        def pick(first, count, where):
            def select(i, held):
                return jnp.where(where == i, scalars[first + i], held)

            return lax.fori_loop(0, count, select, jnp.zeros((1, depth), jnp.float32))

        gap = pick(0, num_cond, band) - pick(num_cond, num_val, orbital)
        norm = math.sqrt(num_cond * num_val)
        first = pl.multiple_of(lax.rem(w, wide // narrow) * (row_width // 2), 128)
        listed = lists[w // (wide // narrow), :, pl.ds(first, rows.shape[1])]
        index = gmap[:, pl.ds(pl.multiple_of(w * row_width, 128), row_width)]
        turned = expand(rows[...], listed, index, num_val).T
        for i in range(num):
            omega = scalars[num_cond + num_val + i]
            weight = -2.0 * gap / (gap * gap + omega * omega) / norm
            scaled[i] = (turned * weight).astype(jnp.bfloat16)

    first = pl.multiple_of(step * (tile // 2), 128)
    here = pl.ds(first, window)
    part = gmap.shape[1] // narrow
    index = gmap[:, pl.ds(pl.multiple_of(n * part + step * tile, 128), tile)]
    panel = expand(columns[:, here], lists[n, :, here], index, num_val).astype(jnp.bfloat16)
    for i in range(num):
        out[i] = dot(scaled[i], panel)


def chi_of(eps_cond, eps_val, omega, gmap, lists, rows, columns, row_width, width, tile, window):
    depth, row_slots = rows.shape
    num = omega.shape[0]
    grant = 4 * depth * (row_slots + columns.shape[1]) + 8 * num * row_width * tile
    grant += (2 * num + 16) * row_width * depth + 16 * depth * tile + (8 << 20)
    scalars = jnp.concatenate([eps_cond, eps_val, omega])
    return pl.pallas_call(
        functools.partial(chi_kernel, eps_cond.shape[0], eps_val.shape[0], window),
        grid=(width // tile,),
        out_shape=jax.ShapeDtypeStruct((num, row_width, width), jnp.float32),
        in_specs=[
            pl.BlockSpec(memory_space=SMEM),
            pl.BlockSpec(gmap.shape, lambda c: (0, 0)),
            pl.BlockSpec(lists.shape, lambda c: (0, 0, 0)),
            pl.BlockSpec(rows.shape, lambda c: (0, 0)),
            pl.BlockSpec(columns.shape, lambda c: (0, 0)),
        ],
        out_specs=pl.BlockSpec((num, row_width, tile), lambda c: (0, 0, c)),
        scratch_shapes=[pltpu.VMEM((num, row_width, depth), jnp.bfloat16)],
        compiler_params=pltpu.CompilerParams(vmem_limit_bytes=min(grant, 60 << 20)),
    )(scalars, gmap, jnp.asarray(lists), rows, columns)


def body(valence, conduction, eps_val, eps_cond, omega, gmap):
    wide, narrow = lax.axis_size("wide"), lax.axis_size("narrow")
    devices = wide * narrow
    num_val = valence.shape[0]
    assert conduction.shape[0] == 1
    plane = GRID * GRID
    waves = gmap.shape[0]
    row_width, width = waves // wide, waves // narrow
    tile = min(512, width)
    lists, windows = half_lists(waves, narrow, (row_width, tile))
    band = conduction.reshape(GRID, 1, plane)
    columns, rows = gather_pairs(
        valence, band, waves, lists, windows[row_width], row_width // 2, wide, narrow
    )
    depth = devices * 2 * num_val
    columns, rows = columns.reshape(depth, -1), rows.reshape(depth, -1)
    spot = gmap.reshape(1, waves)
    return chi_of(
        eps_cond, eps_val, omega, spot, lists, rows, columns, row_width, width, tile, windows[tile]
    )


def solution(mesh):
    placed = (P(None, ("wide", "narrow")), P(("wide", "narrow"), None), P(), P(), P(), P())
    return jax.shard_map(
        body, mesh=mesh, in_specs=placed, out_specs=P(None, "wide", "narrow"), check_vma=False
    )
```

```python
import functools
import math

import jax
import jax.numpy as jnp
import numpy as np
from jax import lax
from jax.experimental import pallas as pl
from jax.experimental.pallas import tpu as pltpu
from jax.sharding import PartitionSpec as P

GRID = 32
MESH = pl.DeviceIdType.MESH
VMEM = pltpu.MemorySpace.VMEM
HBM = pltpu.MemorySpace.HBM
SMEM = pltpu.MemorySpace.SMEM


def wide_factors(wide):
    chips = wide // 2
    inner = 2 ** (int(math.log2(chips)) // 2)
    return chips // inner, inner


@functools.lru_cache(None)
def tables(num_waves, num_val):
    fold = np.arange(GRID)
    fold = np.where(fold < GRID // 2, fold, fold - GRID)
    squares = fold**2
    lengths = (squares[:, None, None] + squares[None, :, None] + squares[None, None, :]).reshape(-1)
    limit = int(np.sort(lengths)[num_waves - 1])
    reach = math.isqrt(limit)
    assert reach < GRID // 2
    half = [
        (ky, kz)
        for ky in range(-reach, reach + 1)
        for kz in range(0, reach + 1)
        if ky * ky + kz * kz <= limit and (kz > 0 or ky >= 0)
    ]
    count = -(-len(half) // 128) * 128
    kys = np.array([k for k, _ in half])
    kzs = np.array([k for _, k in half])
    points = np.arange(GRID)
    turn = 2.0 * np.pi / GRID
    phase = (points[:, None, None] * kys + points[None, :, None] * kzs) % GRID
    phase = phase.reshape(GRID * GRID, len(half)) * turn
    plane = np.zeros((GRID * GRID, 2 * count))
    plane[:, : len(half)] = np.cos(phase)
    plane[:, count : count + len(half)] = -np.sin(phase)
    codes = np.full((count, 2), -1, np.int32)
    codes[: len(half), 0] = (kys % GRID) * GRID + kzs % GRID
    codes[: len(half), 1] = (-kys % GRID) * GRID + -kzs % GRID
    kxs = np.arange(-reach, reach + 1)
    line = (kxs[:, None] * points[None, :] % GRID) * turn
    eye = np.eye(num_val)
    norm = 1.0 / math.sqrt(GRID**3)
    cosine = np.kron(np.cos(line), eye) * norm
    sine = np.kron(np.sin(line), eye) * norm
    return plane, codes, np.stack([cosine, sine]), reach


def round_up(count, step):
    return -(-count // step) * step


@functools.lru_cache(None)
def half_lists(num_waves, narrow, tiles):
    fold = np.arange(GRID)
    fold = np.where(fold < GRID // 2, fold, fold - GRID)
    kx, ky, kz = [k.reshape(-1) for k in np.meshgrid(fold, fold, fold, indexing="ij")]
    lengths = kx * kx + ky * ky + kz * kz
    ordered = np.sort(lengths)[:num_waves]
    half = (kz > 0) | ((kz == 0) & ((ky > 0) | ((ky == 0) & (kx >= 0))))
    chosen = np.nonzero(half & (lengths <= ordered[-1]))[0]
    chosen = chosen[np.argsort(lengths[chosen], kind="stable")]
    sizes = lengths[chosen]
    part = num_waves // narrow
    ends = []
    for n in range(narrow):
        begin = np.searchsorted(sizes, ordered[n * part])
        ends.append((begin, np.searchsorted(sizes, ordered[(n + 1) * part - 1], side="right")))
    below, above = 0, {tile: 0 for tile in tiles}
    for n, (begin, _) in enumerate(ends):
        for tile in tiles:
            for t in range(part // tile):
                g = n * part + t * tile
                low = np.searchsorted(sizes, ordered[g]) - begin - t * tile // 2
                high = np.searchsorted(sizes, ordered[g + tile - 1], side="right") - begin - t * tile // 2
                below, above[tile] = max(below, -int(low)), max(above[tile], int(high))
    windows = {tile: round_up(below + above[tile], 128) for tile in tiles}
    slots = max((part // tile - 1) * tile // 2 + windows[tile] for tile in tiles)
    slots = max(slots, round_up(below + max(end - begin for begin, end in ends), 128))
    lists = np.full((narrow, 1, slots), -1, np.int32)
    for n, (begin, end) in enumerate(ends):
        lists[n, 0, below : below + end - begin] = chosen[begin:end]
    return lists, windows


def np_halves(table):
    table = np.asarray(table, np.float32)
    high = table.astype(jnp.bfloat16)
    return high, (table - high.astype(np.float32)).astype(jnp.bfloat16)


def split_bf16(x):
    high = x.astype(jnp.bfloat16)
    return high, (x - high.astype(jnp.float32)).astype(jnp.bfloat16)


def dot(a, b):
    return jnp.dot(a, b, preferred_element_type=jnp.float32)


def dot3(a, b_high, b_low):
    a_high, a_low = split_bf16(a)
    return dot(a_high, b_high) + (dot(a_low, b_high) + dot(a_high, b_low))


def dot3_left(a_high, a_low, b):
    b_high, b_low = split_bf16(b)
    return dot(a_high, b_high) + (dot(a_high, b_low) + dot(a_low, b_high))


def flip(i, mask, size):
    assert size & (size - 1) == 0
    out, bit = i, 1
    while bit < size:
        if mask & bit:
            out = out + bit * (1 - 2 * lax.rem(i // bit, 2))
        bit *= 2
    return out


class Place:
    def __init__(self, wide, narrow):
        self.outer, self.inner = wide_factors(wide)
        self.wide, self.narrow = wide, narrow
        self.w, self.n = lax.axis_index("wide"), lax.axis_index("narrow")
        self.core = lax.rem(self.w, 2)
        self.y = lax.rem(self.w // 2, self.inner)
        self.z = self.w // (2 * self.inner)
        self.sizes = dict(z=self.outer, y=self.inner, x=narrow)

    def wide_at(self, zz, yy, cc):
        return (zz * self.inner + yy) * 2 + cc

    def slot(self, zz, yy, cc, nn):
        return self.wide_at(zz, yy, cc) * self.narrow + nn

    def moved(self, masks):
        return (
            flip(self.z, masks.get("z", 0), self.outer),
            flip(self.y, masks.get("y", 0), self.inner),
            flip(self.n, masks.get("x", 0), self.narrow),
        )

    def device(self, masks):
        zz, yy, nn = self.moved(masks)
        return (self.wide_at(zz, yy, self.core), nn)

    def peers(self):
        found = []
        for dim, size in self.sizes.items():
            found += [self.device({dim: m}) for m in range(1, size)]
        other = self.wide_at(self.z, self.y, 1 - self.core)
        found += [(other, flip(self.n, m, self.narrow)) for m in range(self.narrow)]
        return found


def count_first(sizes, order):
    a, b, c = [sizes[dim] for dim in order]
    return (a - 1 + b - 1 + c - 1 + 1) + (a - 1) * (b - 1 + c - 1 + 1) + (b - 1) * a * (c - 1 + 1) + (c - 1) * a * b


ORDERS = (("z", "y", "x"), ("z", "x", "y"))


def first_gather(place, order, src, view, send_sem, recv_sem, idle):
    sizes = [place.sizes[dim] for dim in order]
    partner = (place.wide_at(place.z, place.y, 1 - place.core), place.n)
    count = [0]

    def send(ref, index, target):
        pltpu.make_async_remote_copy(
            src_ref=ref,
            dst_ref=view(index),
            send_sem=send_sem.at[count[0]],
            recv_sem=recv_sem.at[index],
            device_id=target,
            device_id_type=MESH,
        ).start()
        count[0] += 1

    def arrived(index):
        pltpu.make_async_remote_copy(
            src_ref=view(index),
            dst_ref=view(index),
            send_sem=send_sem.at[0],
            recv_sem=recv_sem.at[index],
            device_id=partner,
            device_id_type=MESH,
        ).wait_recv()

    def index_of(masks):
        zz, yy, nn = place.moved(masks)
        return place.slot(zz, yy, place.core, nn)

    mine = index_of({})
    for dim, size in zip(order, sizes):
        for m in range(size - 1, 0, -1):
            send(src, mine, place.device({dim: m}))
    send(src, mine, partner)
    idle()
    for level in range(3):
        lower = [{}]
        for dim, size in zip(order[:level], sizes[:level]):
            lower = [{**masks, dim: m} for masks in lower for m in range(size)]
        for m in range(1, sizes[level]):
            for masks in lower:
                index = index_of({**masks, order[level]: m})
                arrived(index)
                for dim, size in zip(order[level + 1 :], sizes[level + 1 :]):
                    for k in range(size - 1, 0, -1):
                        send(view(index), index, place.device({dim: k}))
                send(view(index), index, partner)
    assert count[0] == count_first(place.sizes, order)


def pairs_kernel(wide, narrow, reach, slots, window, row_window, row_step, *refs):
    energies = refs[:3]
    src, sources = refs[3], refs[4:12]
    panel_out, scaled_out = refs[12:14]
    val, held = refs[14], refs[15:23]
    stage, picked, pick_hot, pick_x, pick_sign, local = refs[23:29]
    cols, rows, hot, hot_sign, row_hot, row_sign, weights, panel, scaled = refs[29:38]
    eps_cond, eps_val, omega = refs[38:41]
    first_send, first_recv, own_sem, load_sem, send_sem, recv_sem, row_recv, out_sem = refs[41:49]
    cond, plane_h, plane_l, line_h, line_l, codes, lists, gmap = held
    place = Place(wide, narrow)
    core, n, w, z, y = place.core, place.n, place.w, place.z, place.y
    outer, inner = place.outer, place.inner
    grid, num_val, plane = val.shape
    devices = wide * narrow
    chunk = src.shape[1]
    per = plane // chunk
    count = codes.shape[0]
    kinds = 2 * reach + 1
    size = kinds * num_val

    copies = [pltpu.make_async_copy(a, b, load_sem.at[i]) for i, (a, b) in enumerate(zip([*sources, *energies], [*held, eps_cond, eps_val, omega]))]
    for i in (5, 6, 0, 1, 2, 3, 4, 7, 8, 9, 10):
        copies[i].start()

    peers = place.peers()
    barrier = pltpu.get_barrier_semaphore()
    for peer in peers:
        pl.semaphore_signal(barrier, inc=1, device_id=peer, device_id_type=MESH)
    pl.semaphore_wait(barrier, len(peers))

    def view(index):
        if per == 1:
            return val.at[index]
        return val.at[index // per, :, pl.ds(pl.multiple_of(lax.rem(index, per) * chunk, chunk), chunk)]

    mine = place.slot(z, y, core, n)
    own = pltpu.make_async_copy(src, view(mine), own_sem)
    own.start()

    def prepare():
        copies[5].wait()
        copies[6].wait()
        first, second = codes[:, 0:1], codes[:, 1:2]
        tile = 256 if pick_hot.shape[1] % 256 == 0 else 128

        def body(t, carry):
            here = pl.ds(pl.multiple_of(t * tile, tile), tile)
            index = jnp.maximum(lists[:, here], 0)
            kx = index // (GRID * GRID)
            code = index % (GRID * GRID)
            ky, kz = code // GRID, code % GRID
            kx = jnp.where(kx < GRID // 2, kx, kx - GRID)
            direct = ((kz > 0) & (kz < GRID // 2)) | ((kz == 0) & (ky < GRID // 2))
            pick_x[:, here] = jnp.where(direct, kx, -kx) + reach
            pick_sign[:, here] = jnp.where(direct, 1.0, -1.0).astype(jnp.float32)
            hit = (code == first) | (code == second)
            pick_hot[:, here] = jnp.where(hit, 1.0, 0.0).astype(jnp.bfloat16)
            return carry

        lax.fori_loop(0, pick_hot.shape[1] // tile, body, 0)

    for side in range(2):
        @pl.when(core == side)
        def _():
            first_gather(place, ORDERS[side], src, view, first_send, first_recv, prepare)

    own.wait()
    step = narrow // per

    def flat(cc):
        copies_of = [(2 * q + cc) * step for q in range(wide // 2)]
        field = [(val[pl.ds(p, step)] * cond[pl.ds(p, step)]).reshape(step * num_val, plane) for p in copies_of]
        result = dot3(jnp.concatenate(field, axis=0), plane_h[...], plane_l[...])
        for q, p in enumerate(copies_of):
            part = result[q * step * num_val : (q + 1) * step * num_val]
            stage[pl.ds(p, step)] = part.reshape(step, num_val, 2 * count)

    for i in range(3):
        copies[i].wait()
    flat(core)
    for zz in range(outer):
        for yy in range(inner):
            for nn in range(narrow):
                index = place.slot(zz, yy, 1 - core, nn)
                pltpu.make_async_copy(view(index), view(index), first_recv.at[index]).wait()
    flat(1 - core)
    copies[3].wait()
    copies[4].wait()
    whole = stage[...].reshape(grid * num_val, 2 * count)
    real, imag = whole[:, :count], whole[:, count:]
    cos_h, sin_h, cos_l, sin_l = line_h[0], line_h[1], line_l[0], line_l[1]
    picked[:size, :] = (dot3_left(cos_h, cos_l, real) + dot3_left(sin_h, sin_l, imag)).astype(jnp.bfloat16)
    picked[size:, :] = (dot3_left(cos_h, cos_l, imag) - dot3_left(sin_h, sin_l, real)).astype(jnp.bfloat16)

    def pick(half, store):
        base = pl.multiple_of(half * slots, 128)
        for begin in range(0, slots, 512):
            tile = min(512, slots - begin)
            here = pl.ds(pl.multiple_of(base + begin, 128), tile)
            columns = dot(picked[...], pick_hot[:, here]).reshape(2, kinds, num_val, tile)
            kx = jnp.broadcast_to(pick_x[:, here], (num_val, tile))
            sign = pick_sign[:, here]
            real = jnp.zeros((num_val, tile), jnp.float32)
            imag = jnp.zeros((num_val, tile), jnp.float32)
            for k in range(kinds):
                keep = kx == k
                real = jnp.where(keep, columns[0, k], real)
                imag = jnp.where(keep, columns[1, k], imag)
            store(begin, tile, jnp.concatenate([real, imag * sign], axis=0).astype(jnp.bfloat16))

    partner = (place.wide_at(z, y, 1 - core), n)
    pending = []

    def send(src_ref, dst_ref, target, sem, when=None):
        k = len(pending)
        pltpu.make_async_remote_copy(
            src_ref=src_ref,
            dst_ref=dst_ref,
            send_sem=send_sem.at[k],
            recv_sem=sem,
            device_id=target,
            device_id_type=MESH,
        ).start()
        pending.append((when, src_ref.shape))

    def forward(index, target, when=None):
        send(cols.at[index], cols.at[index], target, recv_sem.at[index], when)

    def arrived(index):
        pltpu.make_async_copy(cols.at[index], cols.at[index], recv_sem.at[index]).wait()

    holder = w // (wide // narrow)
    window_of = lambda ww: pl.multiple_of(lax.rem(ww, wide // narrow) * row_step, 128)
    others = [m for m in range(1, narrow)]

    def row_sends(zz, yy, when):
        start = place.slot(zz, yy, core, 0)
        group = (zz * inner + yy) * 2 + core

        @pl.when(n == holder)
        def _():
            for cc in (core, 1 - core):
                ww = place.wide_at(z, y, cc)
                for m in others:
                    send(
                        cols.at[pl.ds(start, narrow), :, pl.ds(window_of(ww), row_window)],
                        rows.at[pl.ds(start, narrow)],
                        (ww, flip(n, m, narrow)),
                        row_recv.at[group],
                        (when, "row"),
                    )

    block = devices // outer
    block_rows = block * 2 * num_val
    tile = hot.shape[2]

    def prepare_hot():
        for copy in copies[7:]:
            copy.wait()
        num_cond, num = eps_cond.shape[0], omega.shape[0]
        depth = panel.shape[0]
        lane = lax.broadcasted_iota(jnp.int32, (1, depth), 1)
        band, orbital = lane // (2 * num_val), lane % num_val

        def choose(ref, where):
            def select(i, held):
                return jnp.where(where == i, ref[i], held)

            return lax.fori_loop(0, ref.shape[0], select, jnp.zeros((1, depth), jnp.float32))

        gap = choose(eps_cond, band) - choose(eps_val, orbital)
        norm = math.sqrt(num_cond * num_val)
        for i in range(num):
            weights[i : i + 1, :] = -2.0 * gap / (gap * gap + omega[i] * omega[i]) / norm

        row_width = row_hot.shape[1]
        first = pl.multiple_of(holder * slots + lax.rem(w, wide // narrow) * row_step, 128)
        index = gmap[:, pl.ds(pl.multiple_of(w * row_width, 128), row_width)]
        row_hot[...], row_sign[...] = expansion(lists[:, pl.ds(first, row_window)], index)

        def body(t, carry):
            first = pl.multiple_of(n * slots + t * (tile // 2), 128)
            here = pl.ds(pl.multiple_of(t * tile, 128), tile)
            index = gmap[:, pl.ds(pl.multiple_of(n * (tile * hot.shape[0]) + t * tile, 128), tile)]
            hot[t], hot_sign[:, here] = expansion(lists[:, pl.ds(first, window)], index)
            return carry

        lax.fori_loop(0, hot.shape[0], body, 0)

    def signed(values, sign):
        row = lax.broadcasted_iota(jnp.int32, values.shape, 0)
        return values * jnp.where(row // num_val % 2 == 1, sign, 1.0)

    def expand_block(zz):
        first = zz * block
        base = pl.multiple_of(zz * block_rows, 16)
        for yy in range(inner):
            for nn in range(narrow):
                arrived(place.slot(zz, yy, 1 - core, nn))

        def body(t, carry):
            source = cols[pl.ds(first, block), :, pl.ds(pl.multiple_of(t * (tile // 2), 128), window)]
            here = pl.ds(pl.multiple_of(t * tile, 128), tile)
            values = dot(source.reshape(block_rows, window), hot[t])
            panel[pl.ds(base, block_rows), here] = signed(values, hot_sign[:, here]).astype(jnp.bfloat16)
            return carry

        lax.fori_loop(0, hot.shape[0], body, 0)
        block_copies(zz)[0].start()

    def block_copies(zz):
        here = pl.ds(pl.multiple_of(zz * block_rows, 128), block_rows)
        return (
            pltpu.make_async_copy(panel.at[here], panel_out.at[here], out_sem.at[0, zz]),
            pltpu.make_async_copy(scaled.at[:, :, here], scaled_out.at[:, :, here], out_sem.at[1, zz]),
        )

    def scale_block(zz):
        first = zz * block
        here = pl.ds(pl.multiple_of(zz * block_rows, 128), block_rows)

        @pl.when(n == holder)
        def _():
            rows[pl.ds(first, block)] = cols[pl.ds(first, block), :, pl.ds(window_of(w), row_window)]

        @pl.when(n != holder)
        def _():
            for group in range(block // narrow):
                rows_of = rows.at[pl.ds(first + group * narrow, narrow)]
                pltpu.make_async_copy(rows_of, rows_of, row_recv.at[zz * (block // narrow) + group]).wait()

        values = dot(rows[pl.ds(first, block)].reshape(block_rows, row_window), row_hot[...])
        turned = signed(values, row_sign[...]).T
        for i in range(scaled.shape[0]):
            scaled[i, :, here] = (turned * weights[i : i + 1, here]).astype(jnp.bfloat16)
        block_copies(zz)[1].start()

    for m in range(narrow - 1, 0, -1):
        half = flip(n, m, narrow)

        def store(begin, tile, value, m=m):
            local[m - 1, :, begin : begin + tile] = value

        pick(half, store)
        send(local.at[m - 1], cols.at[mine], (w, half), recv_sem.at[mine])

    def store_own(begin, tile, value):
        cols[mine, :, begin : begin + tile] = value

    pick(n, store_own)
    right, left = (place.wide_at(z + 1, y, core), n), (place.wide_at(z - 1, y, core), n)

    def spread(index, when, go_right, go_left):
        if go_right:
            @pl.when(z < outer - 1)
            def _():
                forward(index, right, (when, "right"))
        if go_left:
            @pl.when(z > 0)
            def _():
                forward(index, left, (when, "left"))
        for m in range(1, inner):
            forward(index, place.device({"y": m}), (when, None))
        forward(index, partner, (when, None))

    spread(mine, None, True, True)
    prepare_hot()
    for m in others:
        index = place.slot(z, y, core, flip(n, m, narrow))
        arrived(index)
        spread(index, None, True, True)
    row_sends(z, y, None)

    def side_blocks(zz, when):
        for m in range(1, inner):
            yy = flip(y, m, inner)
            for k in range(narrow):
                index = place.slot(zz, yy, core, flip(n, k, narrow))
                arrived(index)
                forward(index, partner, (when, None))
            row_sends(zz, yy, when)

    def present(offset):
        return (z + offset >= 0) & (z + offset < outer)

    def each(s, work):
        if s == 0:
            work(z, None)
            return
        for offset in (-s, s):
            @pl.when(present(offset))
            def _():
                work(z + offset, offset)

    def line_blocks(zz, offset):
        for k in range(narrow):
            index = place.slot(zz, y, core, flip(n, k, narrow))
            arrived(index)
            spread(index, offset, offset < 0, offset > 0)
        row_sends(zz, y, offset)

    for s in range(1, outer + 2):
        if s < outer:
            each(s, line_blocks)
        if s - 1 < outer:
            each(s - 1, side_blocks)
        if s >= 2:
            each(s - 2, lambda zz, offset: expand_block(zz))
            each(s - 2, lambda zz, offset: scale_block(zz))

    for zz in range(outer):
        for copy in block_copies(zz):
            copy.wait()

    def drain(k, shape):
        ref = cols.at[0] if len(shape) == 2 else rows.at[pl.ds(0, narrow)]
        pltpu.make_async_copy(ref, ref, send_sem.at[k]).wait()

    waits = {}
    for k, (when, shape) in enumerate(pending):
        when = when if isinstance(when, tuple) else (when, None)
        waits.setdefault(when, []).append((k, shape))
    for (offset, kind), items in waits.items():
        test = None
        if offset is not None:
            test = present(offset)
        extra = {"right": z < outer - 1, "left": z > 0, "row": n == holder}.get(kind)
        if extra is not None:
            test = extra if test is None else test & extra

        def all_of(items=items):
            for k, shape in items:
                drain(k, shape)

        if test is None:
            all_of()
        else:
            pl.when(test)(all_of)

    for side, order in enumerate(ORDERS):
        @pl.when(core == side)
        def _():
            for k in range(count_first(place.sizes, order)):
                pltpu.make_async_copy(src, src, first_send.at[k]).wait()


def second_sends(outer, inner, narrow):
    spread = 2 + (inner - 1) + 1
    row = 2 * (narrow - 1)
    sides = (inner - 1) * (narrow + row)
    total = narrow - 1 + narrow * spread + row + sides
    return total + 2 * (outer - 1) * (narrow * (spread - 1) + row + sides)


def gather_pairs(val, cond, gmap, energies, lists, window, row_window, row_width, tile, wide, narrow):
    num_val, chunk = val.shape
    waves = gmap.shape[1]
    table, codes, line, reach = tables(waves, num_val)
    plane_h, plane_l = np_halves(table)
    line_h, line_l = np_halves(line)
    slots = lists.shape[2]
    outer, inner = wide_factors(wide)
    devices = wide * narrow
    count = codes.shape[0]
    plane = GRID * GRID
    kinds = 2 * reach + 1
    operands = (cond, plane_h, plane_l, line_h, line_l, codes, lists.reshape(1, -1), gmap)
    held = [pltpu.VMEM(x.shape, x.dtype) for x in operands]
    sizes = dict(z=outer, y=inner, x=narrow)
    sends = max(count_first(sizes, order) for order in ORDERS)
    depth = 2 * num_val
    width = waves // narrow
    num = energies[2].shape[0]
    return pl.pallas_call(
        functools.partial(pairs_kernel, wide, narrow, reach, slots, window, row_window, row_width // 2),
        out_shape=[
            jax.ShapeDtypeStruct((devices * depth, width), jnp.bfloat16),
            jax.ShapeDtypeStruct((num, row_width, devices * depth), jnp.bfloat16),
        ],
        in_specs=[pl.BlockSpec(memory_space=HBM)] * 12,
        out_specs=[pl.BlockSpec(memory_space=HBM)] * 2,
        scratch_shapes=[pltpu.VMEM((GRID, num_val, plane), jnp.float32)]
        + held
        + [
            pltpu.VMEM((GRID, num_val, 2 * count), jnp.float32),
            pltpu.VMEM((2 * kinds * num_val, count), jnp.bfloat16),
            pltpu.VMEM((count, narrow * slots), jnp.bfloat16),
            pltpu.VMEM((1, narrow * slots), jnp.int32),
            pltpu.VMEM((1, narrow * slots), jnp.float32),
            pltpu.VMEM((narrow - 1, depth, slots), jnp.bfloat16),
            pltpu.VMEM((devices, depth, slots), jnp.bfloat16),
            pltpu.VMEM((devices, depth, row_window), jnp.bfloat16),
            pltpu.VMEM((width // tile, window, tile), jnp.bfloat16),
            pltpu.VMEM((1, width), jnp.float32),
            pltpu.VMEM((row_window, row_width), jnp.bfloat16),
            pltpu.VMEM((1, row_width), jnp.float32),
            pltpu.VMEM((num, devices * depth), jnp.float32),
            pltpu.VMEM((devices * depth, width), jnp.bfloat16),
            pltpu.VMEM((num, row_width, devices * depth), jnp.bfloat16),
        ]
        + [pltpu.SMEM(x.shape, x.dtype) for x in energies]
        + [
            pltpu.SemaphoreType.DMA((sends,)),
            pltpu.SemaphoreType.DMA((devices,)),
            pltpu.SemaphoreType.DMA,
            pltpu.SemaphoreType.DMA((11,)),
            pltpu.SemaphoreType.DMA((second_sends(outer, inner, narrow),)),
            pltpu.SemaphoreType.DMA((devices,)),
            pltpu.SemaphoreType.DMA((wide,)),
            pltpu.SemaphoreType.DMA((2, outer)),
        ],
        compiler_params=pltpu.CompilerParams(
            collective_id=0, has_side_effects=True, vmem_limit_bytes=63 << 20
        ),
    )(*energies, val, *[jnp.asarray(x) for x in operands])


def expansion(listed, index):
    slots, tile = listed.shape[1], index.shape[1]
    area = GRID * GRID
    lx, ly, lz = listed // area, listed // GRID % GRID, listed % GRID
    mirror = (GRID - lx) % GRID * area + (GRID - ly) % GRID * GRID + (GRID - lz) % GRID
    mirror = jnp.where(listed < 0, -1, mirror)

    def column(row):
        turned = jnp.broadcast_to(row, (128, slots)).T
        return jnp.concatenate([turned] * (tile // 128), axis=1)

    hit = (index == column(listed)) | (index == column(mirror))
    kx, ky, kz = index // area, index // GRID % GRID, index % GRID
    low = GRID // 2
    direct = ((kz > 0) & (kz < low)) | (
        (kz == 0) & (((ky > 0) & (ky < low)) | ((ky == 0) & (kx < low)))
    )
    sign = jnp.where(direct, 1.0, -1.0).astype(jnp.float32)
    return jnp.where(hit, 1.0, 0.0).astype(jnp.bfloat16), sign


def chi_kernel(tile, scaled_src, panel_src, out, scaled, panel, held, scaled_sem, panel_sem, sems):
    num, row_width, depth = scaled.shape
    steps = panel.shape[0]

    def load(t):
        here = pl.ds(pl.multiple_of(t * tile, 128), tile)
        return pltpu.make_async_copy(panel_src.at[:, here], panel.at[t], panel_sem.at[t])

    def take(i):
        return pltpu.make_async_copy(scaled_src.at[i], scaled.at[i], scaled_sem.at[i])

    def copy(slot, i, t):
        here = pl.ds(pl.multiple_of(t * tile, 128), tile)
        return pltpu.make_async_copy(held.at[slot, i], out.at[i, :, here], sems.at[slot, i])

    load(0).start()
    for i in range(num):
        take(i).start()
    for t in range(1, steps):
        load(t).start()
    load(0).wait()
    for i in range(num):
        take(i).wait()
        held[0, i] = dot(scaled[i], panel[0])
        copy(0, i, 0).start()

    def body(t, carry):
        slot = lax.rem(t, 2)
        load(t).wait()

        @pl.when(t >= 2)
        def _():
            for i in range(num):
                copy(slot, i, t - 2).wait()

        for i in range(num):
            held[slot, i] = dot(scaled[i], panel[t])
        for i in range(num):
            copy(slot, i, t).start()
        return carry

    lax.fori_loop(1, steps, body, 0)
    for t in range(max(0, steps - 2), steps):
        for i in range(num):
            copy(t % 2, i, t).wait()


def chi_of(scaled, panel, tile):
    num, row_width, depth = scaled.shape
    width = panel.shape[1]
    return pl.pallas_call(
        functools.partial(chi_kernel, tile),
        out_shape=jax.ShapeDtypeStruct((num, row_width, width), jnp.float32),
        in_specs=[pl.BlockSpec(memory_space=HBM)] * 2,
        out_specs=pl.BlockSpec(memory_space=HBM),
        scratch_shapes=[
            pltpu.VMEM(scaled.shape, jnp.bfloat16),
            pltpu.VMEM((width // tile, depth, tile), jnp.bfloat16),
            pltpu.VMEM((2, num, row_width, tile), jnp.float32),
            pltpu.SemaphoreType.DMA((num,)),
            pltpu.SemaphoreType.DMA((width // tile,)),
            pltpu.SemaphoreType.DMA((2, num)),
        ],
        compiler_params=pltpu.CompilerParams(vmem_limit_bytes=63 << 20),
    )(scaled, panel)


def body(valence, conduction, eps_val, eps_cond, omega, gmap):
    wide, narrow = lax.axis_size("wide"), lax.axis_size("narrow")
    assert conduction.shape[0] == 1
    waves = gmap.shape[0]
    row_width, width = waves // wide, waves // narrow
    tile = min(512, width)
    lists, windows = half_lists(waves, narrow, (row_width, tile))
    band = conduction.reshape(GRID, 1, GRID * GRID)
    energies = (eps_cond, eps_val, omega)
    panel, scaled = gather_pairs(
        valence, band, gmap.reshape(1, waves), energies, lists, windows[tile], windows[row_width],
        row_width, tile, wide, narrow,
    )
    return chi_of(scaled, panel, tile)


def solution(mesh):
    placed = (P(None, ("wide", "narrow")), P(("wide", "narrow"), None), P(), P(), P(), P())
    return jax.shard_map(
        body, mesh=mesh, in_specs=placed, out_specs=P(None, "wide", "narrow"), check_vma=False
    )
```

```python
import functools
import math

import jax
import jax.numpy as jnp
import numpy as np
from jax import lax
from jax.experimental import pallas as pl
from jax.experimental.pallas import tpu as pltpu
from jax.sharding import PartitionSpec as P

GRID = 32
MESH = pl.DeviceIdType.MESH
VMEM = pltpu.MemorySpace.VMEM
HBM = pltpu.MemorySpace.HBM
SMEM = pltpu.MemorySpace.SMEM


def wide_factors(wide):
    chips = wide // 2
    inner = 2 ** (int(math.log2(chips)) // 2)
    return chips // inner, inner


@functools.lru_cache(None)
def tables(num_waves, num_val):
    fold = np.arange(GRID)
    fold = np.where(fold < GRID // 2, fold, fold - GRID)
    squares = fold**2
    lengths = (squares[:, None, None] + squares[None, :, None] + squares[None, None, :]).reshape(-1)
    limit = int(np.sort(lengths)[num_waves - 1])
    reach = math.isqrt(limit)
    assert reach < GRID // 2
    half = [
        (ky, kz)
        for ky in range(-reach, reach + 1)
        for kz in range(0, reach + 1)
        if ky * ky + kz * kz <= limit and (kz > 0 or ky >= 0)
    ]
    count = -(-len(half) // 128) * 128
    kys = np.array([k for k, _ in half])
    kzs = np.array([k for _, k in half])
    points = np.arange(GRID)
    turn = 2.0 * np.pi / GRID
    phase = (points[:, None, None] * kys + points[None, :, None] * kzs) % GRID
    phase = phase.reshape(GRID * GRID, len(half)) * turn
    plane = np.zeros((GRID * GRID, 2 * count))
    plane[:, : len(half)] = np.cos(phase)
    plane[:, count : count + len(half)] = -np.sin(phase)
    codes = np.full((count, 2), -1, np.int32)
    codes[: len(half), 0] = (kys % GRID) * GRID + kzs % GRID
    codes[: len(half), 1] = (-kys % GRID) * GRID + -kzs % GRID
    kxs = np.arange(-reach, reach + 1)
    line = (kxs[:, None] * points[None, :] % GRID) * turn
    eye = np.eye(num_val)
    norm = 1.0 / math.sqrt(GRID**3)
    cosine = np.kron(np.cos(line), eye) * norm
    sine = np.kron(np.sin(line), eye) * norm
    return plane, codes, np.stack([cosine, sine]), reach


def round_up(count, step):
    return -(-count // step) * step


@functools.lru_cache(None)
def half_lists(num_waves, narrow, tiles):
    fold = np.arange(GRID)
    fold = np.where(fold < GRID // 2, fold, fold - GRID)
    kx, ky, kz = [k.reshape(-1) for k in np.meshgrid(fold, fold, fold, indexing="ij")]
    lengths = kx * kx + ky * ky + kz * kz
    ordered = np.sort(lengths)[:num_waves]
    half = (kz > 0) | ((kz == 0) & ((ky > 0) | ((ky == 0) & (kx >= 0))))
    chosen = np.nonzero(half & (lengths <= ordered[-1]))[0]
    chosen = chosen[np.argsort(lengths[chosen], kind="stable")]
    sizes = lengths[chosen]
    part = num_waves // narrow
    ends = []
    for n in range(narrow):
        begin = np.searchsorted(sizes, ordered[n * part])
        ends.append((begin, np.searchsorted(sizes, ordered[(n + 1) * part - 1], side="right")))
    below, above = 0, {tile: 0 for tile in tiles}
    for n, (begin, _) in enumerate(ends):
        for tile in tiles:
            for t in range(part // tile):
                g = n * part + t * tile
                low = np.searchsorted(sizes, ordered[g]) - begin - t * tile // 2
                high = np.searchsorted(sizes, ordered[g + tile - 1], side="right") - begin - t * tile // 2
                below, above[tile] = max(below, -int(low)), max(above[tile], int(high))
    windows = {tile: round_up(below + above[tile], 128) for tile in tiles}
    slots = max((part // tile - 1) * tile // 2 + windows[tile] for tile in tiles)
    slots = max(slots, round_up(below + max(end - begin for begin, end in ends), 128))
    lists = np.full((narrow, 1, slots), -1, np.int32)
    for n, (begin, end) in enumerate(ends):
        lists[n, 0, below : below + end - begin] = chosen[begin:end]
    return lists, windows


def np_halves(table):
    table = np.asarray(table, np.float32)
    high = table.astype(jnp.bfloat16)
    return high, (table - high.astype(np.float32)).astype(jnp.bfloat16)


def split_bf16(x):
    high = x.astype(jnp.bfloat16)
    return high, (x - high.astype(jnp.float32)).astype(jnp.bfloat16)


def dot(a, b):
    return jnp.dot(a, b, preferred_element_type=jnp.float32)


def dot3(a, b_high, b_low):
    a_high, a_low = split_bf16(a)
    return dot(a_high, b_high) + (dot(a_low, b_high) + dot(a_high, b_low))


def dot3_left(a_high, a_low, b):
    b_high, b_low = split_bf16(b)
    return dot(a_high, b_high) + (dot(a_high, b_low) + dot(a_low, b_high))


def flip(i, mask, size):
    assert size & (size - 1) == 0
    out, bit = i, 1
    while bit < size:
        if mask & bit:
            out = out + bit * (1 - 2 * lax.rem(i // bit, 2))
        bit *= 2
    return out


class Place:
    def __init__(self, wide, narrow):
        self.outer, self.inner = wide_factors(wide)
        self.wide, self.narrow = wide, narrow
        self.w, self.n = lax.axis_index("wide"), lax.axis_index("narrow")
        self.core = lax.rem(self.w, 2)
        self.y = lax.rem(self.w // 2, self.inner)
        self.z = self.w // (2 * self.inner)
        self.sizes = dict(z=self.outer, y=self.inner, x=narrow)

    def wide_at(self, zz, yy, cc):
        return (zz * self.inner + yy) * 2 + cc

    def slot(self, zz, yy, cc, nn):
        return self.wide_at(zz, yy, cc) * self.narrow + nn

    def moved(self, masks):
        return (
            flip(self.z, masks.get("z", 0), self.outer),
            flip(self.y, masks.get("y", 0), self.inner),
            flip(self.n, masks.get("x", 0), self.narrow),
        )

    def device(self, masks):
        zz, yy, nn = self.moved(masks)
        return (self.wide_at(zz, yy, self.core), nn)

    def peers(self):
        found = []
        for dim, size in self.sizes.items():
            found += [self.device({dim: m}) for m in range(1, size)]
        other = self.wide_at(self.z, self.y, 1 - self.core)
        found += [(other, flip(self.n, m, self.narrow)) for m in range(self.narrow)]
        for m in range(1, self.narrow):
            for dim in ("y", "z"):
                found += [self.device({dim: k, "x": m}) for k in range(1, self.sizes[dim])]
        return found


def count_first(outer, plane):
    return (outer - 1 + plane) + (outer - 1) * plane + (plane - 1) * outer


def first_gather(place, src, view, send_sem, recv_sem, idle):
    outer, inner, narrow = place.outer, place.inner, place.narrow
    partner = (place.wide_at(place.z, place.y, 1 - place.core), place.n)
    around = [{"y": a, "x": b} for a in range(inner) for b in range(narrow) if a or b]
    around.sort(key=lambda masks: -(masks["y"] > 0) - (masks["x"] > 0))
    count = [0]

    def send(ref, index, target):
        pltpu.make_async_remote_copy(
            src_ref=ref,
            dst_ref=view(index),
            send_sem=send_sem.at[count[0]],
            recv_sem=recv_sem.at[index],
            device_id=target,
            device_id_type=MESH,
        ).start()
        count[0] += 1

    def arrived(index):
        pltpu.make_async_copy(view(index), view(index), recv_sem.at[index]).wait()

    def index_of(masks):
        zz, yy, nn = place.moved(masks)
        return place.slot(zz, yy, place.core, nn)

    mine = index_of({})
    for m in range(outer - 1, 0, -1):
        send(src, mine, place.device({"z": m}))
    for masks in around:
        send(src, mine, place.device(masks))
    send(src, mine, partner)
    idle()
    for m in range(1, outer):
        index = index_of({"z": m})
        arrived(index)
        for masks in around:
            send(view(index), index, place.device(masks))
        send(view(index), index, partner)
    for m in range(outer):
        for masks in around:
            index = index_of({**masks, "z": m})
            arrived(index)
            send(view(index), index, partner)
    assert count[0] == count_first(outer, inner * narrow)


def pairs_kernel(wide, narrow, reach, slots, window, row_window, row_step, *refs):
    energies = refs[:3]
    src, sources = refs[3], refs[4:12]
    panel, scaled = refs[12:14]
    val, held = refs[14], refs[15:23]
    stage, picked, pick_hot, pick_x, pick_sign, local = refs[23:29]
    cols, rows, hot, hot_sign, row_hot, row_sign, weights = refs[29:36]
    eps_cond, eps_val, omega = refs[36:39]
    first_send, first_recv, own_sem, load_sem, send_sem, recv_sem, row_recv = refs[39:46]
    cond, plane_h, plane_l, line_h, line_l, codes, lists, gmap = held
    place = Place(wide, narrow)
    core, n, w, z, y = place.core, place.n, place.w, place.z, place.y
    outer, inner = place.outer, place.inner
    grid, num_val, plane = val.shape
    devices = wide * narrow
    chunk = src.shape[1]
    per = plane // chunk
    count = codes.shape[0]
    kinds = 2 * reach + 1
    size = kinds * num_val

    copies = [pltpu.make_async_copy(a, b, load_sem.at[i]) for i, (a, b) in enumerate(zip([*sources, *energies], [*held, eps_cond, eps_val, omega]))]
    for i in (5, 6, 0, 1, 2, 3, 4, 7, 8, 9, 10):
        copies[i].start()

    peers = place.peers()
    barrier = pltpu.get_barrier_semaphore()
    for peer in peers:
        pl.semaphore_signal(barrier, inc=1, device_id=peer, device_id_type=MESH)
    pl.semaphore_wait(barrier, len(peers))

    def view(index):
        if per == 1:
            return val.at[index]
        return val.at[index // per, :, pl.ds(pl.multiple_of(lax.rem(index, per) * chunk, chunk), chunk)]

    mine = place.slot(z, y, core, n)
    own = pltpu.make_async_copy(src, view(mine), own_sem)
    own.start()

    def prepare():
        copies[5].wait()
        copies[6].wait()
        first, second = codes[:, 0:1], codes[:, 1:2]
        tile = 256 if pick_hot.shape[1] % 256 == 0 else 128

        def body(t, carry):
            here = pl.ds(pl.multiple_of(t * tile, tile), tile)
            index = jnp.maximum(lists[:, here], 0)
            kx = index // (GRID * GRID)
            code = index % (GRID * GRID)
            ky, kz = code // GRID, code % GRID
            kx = jnp.where(kx < GRID // 2, kx, kx - GRID)
            direct = ((kz > 0) & (kz < GRID // 2)) | ((kz == 0) & (ky < GRID // 2))
            pick_x[:, here] = jnp.where(direct, kx, -kx) + reach
            pick_sign[:, here] = jnp.where(direct, 1.0, -1.0).astype(jnp.float32)
            hit = (code == first) | (code == second)
            pick_hot[:, here] = jnp.where(hit, 1.0, 0.0).astype(jnp.bfloat16)
            return carry

        lax.fori_loop(0, pick_hot.shape[1] // tile, body, 0)

    first_gather(place, src, view, first_send, first_recv, prepare)

    own.wait()
    step = narrow // per

    def flat(cc):
        copies_of = [(2 * q + cc) * step for q in range(wide // 2)]
        field = [(val[pl.ds(p, step)] * cond[pl.ds(p, step)]).reshape(step * num_val, plane) for p in copies_of]
        result = dot3(jnp.concatenate(field, axis=0), plane_h[...], plane_l[...])
        for q, p in enumerate(copies_of):
            part = result[q * step * num_val : (q + 1) * step * num_val]
            stage[pl.ds(p, step)] = part.reshape(step, num_val, 2 * count)

    for i in range(3):
        copies[i].wait()
    flat(core)
    for zz in range(outer):
        for yy in range(inner):
            for nn in range(narrow):
                index = place.slot(zz, yy, 1 - core, nn)
                pltpu.make_async_copy(view(index), view(index), first_recv.at[index]).wait()
    flat(1 - core)
    copies[3].wait()
    copies[4].wait()
    whole = stage[...].reshape(grid * num_val, 2 * count)
    real, imag = whole[:, :count], whole[:, count:]
    cos_h, sin_h, cos_l, sin_l = line_h[0], line_h[1], line_l[0], line_l[1]
    picked[:size, :] = (dot3_left(cos_h, cos_l, real) + dot3_left(sin_h, sin_l, imag)).astype(jnp.bfloat16)
    picked[size:, :] = (dot3_left(cos_h, cos_l, imag) - dot3_left(sin_h, sin_l, real)).astype(jnp.bfloat16)

    def pick(half, store):
        base = pl.multiple_of(half * slots, 128)
        for begin in range(0, slots, 512):
            tile = min(512, slots - begin)
            here = pl.ds(pl.multiple_of(base + begin, 128), tile)
            columns = dot(picked[...], pick_hot[:, here]).reshape(2, kinds, num_val, tile)
            kx = jnp.broadcast_to(pick_x[:, here], (num_val, tile))
            sign = pick_sign[:, here]
            real = jnp.zeros((num_val, tile), jnp.float32)
            imag = jnp.zeros((num_val, tile), jnp.float32)
            for k in range(kinds):
                keep = kx == k
                real = jnp.where(keep, columns[0, k], real)
                imag = jnp.where(keep, columns[1, k], imag)
            store(begin, tile, jnp.concatenate([real, imag * sign], axis=0).astype(jnp.bfloat16))

    partner = (place.wide_at(z, y, 1 - core), n)
    pending = []

    def send(src_ref, dst_ref, target, sem, when=None):
        k = len(pending)
        pltpu.make_async_remote_copy(
            src_ref=src_ref,
            dst_ref=dst_ref,
            send_sem=send_sem.at[k],
            recv_sem=sem,
            device_id=target,
            device_id_type=MESH,
        ).start()
        pending.append((when, src_ref.shape))

    def forward(index, target, when=None):
        send(cols.at[index], cols.at[index], target, recv_sem.at[index], when)

    def arrived(index):
        pltpu.make_async_copy(cols.at[index], cols.at[index], recv_sem.at[index]).wait()

    holder = w // (wide // narrow)
    window_of = lambda ww: pl.multiple_of(lax.rem(ww, wide // narrow) * row_step, 128)
    others = [m for m in range(1, narrow)]

    def row_sends(zz, yy, when):
        start = place.slot(zz, yy, core, 0)
        group = (zz * inner + yy) * 2 + core

        @pl.when(n == holder)
        def _():
            for cc in (core, 1 - core):
                ww = place.wide_at(z, y, cc)
                for m in others:
                    send(
                        cols.at[pl.ds(start, narrow), :, pl.ds(window_of(ww), row_window)],
                        rows.at[pl.ds(start, narrow)],
                        (ww, flip(n, m, narrow)),
                        row_recv.at[group],
                        (when, "row"),
                    )

    block = devices // outer
    block_rows = block * 2 * num_val
    tile = hot.shape[2]

    def prepare_hot():
        for copy in copies[7:]:
            copy.wait()
        num_cond, num = eps_cond.shape[0], omega.shape[0]
        depth = panel.shape[0]
        lane = lax.broadcasted_iota(jnp.int32, (1, depth), 1)
        band, orbital = lane // (2 * num_val), lane % num_val

        def choose(ref, where):
            def select(i, held):
                return jnp.where(where == i, ref[i], held)

            return lax.fori_loop(0, ref.shape[0], select, jnp.zeros((1, depth), jnp.float32))

        gap = choose(eps_cond, band) - choose(eps_val, orbital)
        norm = math.sqrt(num_cond * num_val)
        for i in range(num):
            weights[i : i + 1, :] = -2.0 * gap / (gap * gap + omega[i] * omega[i]) / norm

        row_width = row_hot.shape[1]
        first = pl.multiple_of(holder * slots + lax.rem(w, wide // narrow) * row_step, 128)
        index = gmap[:, pl.ds(pl.multiple_of(w * row_width, 128), row_width)]
        row_hot[...], row_sign[...] = expansion(lists[:, pl.ds(first, row_window)], index)

        def body(t, carry):
            first = pl.multiple_of(n * slots + t * (tile // 2), 128)
            here = pl.ds(pl.multiple_of(t * tile, 128), tile)
            index = gmap[:, pl.ds(pl.multiple_of(n * (tile * hot.shape[0]) + t * tile, 128), tile)]
            hot[t], hot_sign[:, here] = expansion(lists[:, pl.ds(first, window)], index)
            return carry

        lax.fori_loop(0, hot.shape[0], body, 0)

    def signed(values, sign):
        row = lax.broadcasted_iota(jnp.int32, values.shape, 0)
        return values * jnp.where(row // num_val % 2 == 1, sign, 1.0)

    def expand_block(zz):
        first = zz * block
        base = pl.multiple_of(zz * block_rows, 16)
        for yy in range(inner):
            for nn in range(narrow):
                arrived(place.slot(zz, yy, 1 - core, nn))

        def body(t, carry):
            source = cols[pl.ds(first, block), :, pl.ds(pl.multiple_of(t * (tile // 2), 128), window)]
            here = pl.ds(pl.multiple_of(t * tile, 128), tile)
            values = dot(source.reshape(block_rows, window), hot[t])
            panel[pl.ds(base, block_rows), here] = signed(values, hot_sign[:, here]).astype(jnp.bfloat16)
            return carry

        lax.fori_loop(0, hot.shape[0], body, 0, unroll=4)

    def scale_block(zz):
        first = zz * block
        here = pl.ds(pl.multiple_of(zz * block_rows, 128), block_rows)

        @pl.when(n == holder)
        def _():
            rows[pl.ds(first, block)] = cols[pl.ds(first, block), :, pl.ds(window_of(w), row_window)]

        @pl.when(n != holder)
        def _():
            for group in range(block // narrow):
                rows_of = rows.at[pl.ds(first + group * narrow, narrow)]
                pltpu.make_async_copy(rows_of, rows_of, row_recv.at[zz * (block // narrow) + group]).wait()

        values = dot(rows[pl.ds(first, block)].reshape(block_rows, row_window), row_hot[...])
        turned = signed(values, row_sign[...]).T
        for i in range(scaled.shape[0]):
            scaled[i, :, here] = (turned * weights[i : i + 1, here]).astype(jnp.bfloat16)

    for m in range(narrow - 1, 0, -1):
        half = flip(n, m, narrow)

        def store(begin, tile, value, m=m):
            local[m - 1, :, begin : begin + tile] = value

        pick(half, store)
        piece = local.at[m - 1]
        send(piece, cols.at[mine], (w, half), recv_sem.at[mine])
        for k in range(1, inner):
            send(piece, cols.at[mine], place.device({"y": k, "x": m}), recv_sem.at[mine])

        @pl.when(z < outer - 1)
        def _():
            send(piece, cols.at[mine], (place.wide_at(z + 1, y, core), half), recv_sem.at[mine], (None, "right"))

        @pl.when(z > 0)
        def _():
            send(piece, cols.at[mine], (place.wide_at(z - 1, y, core), half), recv_sem.at[mine], (None, "left"))


    def store_own(begin, tile, value):
        cols[mine, :, begin : begin + tile] = value

    pick(n, store_own)
    right, left = (place.wide_at(z + 1, y, core), n), (place.wide_at(z - 1, y, core), n)

    def spread(index, when, go_right, go_left):
        if go_right:
            @pl.when(z < outer - 1)
            def _():
                forward(index, right, (when, "right"))
        if go_left:
            @pl.when(z > 0)
            def _():
                forward(index, left, (when, "left"))
        for m in range(1, inner):
            forward(index, place.device({"y": m}), (when, None))
        forward(index, partner, (when, None))

    spread(mine, None, True, True)
    prepare_hot()
    for m in others:
        index = place.slot(z, y, core, flip(n, m, narrow))
        arrived(index)
        forward(index, partner)
    row_sends(z, y, None)

    def side_blocks(zz, when):
        for m in range(1, inner):
            yy = flip(y, m, inner)
            for k in range(narrow):
                index = place.slot(zz, yy, core, flip(n, k, narrow))
                arrived(index)
                forward(index, partner, (when, None))
            row_sends(zz, yy, when)

    def present(offset):
        return (z + offset >= 0) & (z + offset < outer)

    def each(s, work):
        if s == 0:
            work(z, None)
            return
        for offset in (-s, s):
            @pl.when(present(offset))
            def _():
                work(z + offset, offset)

    def line_blocks(zz, offset):
        for k in range(narrow):
            index = place.slot(zz, y, core, flip(n, k, narrow))
            arrived(index)
            spread(index, offset, offset < 0, offset > 0)
        row_sends(zz, y, offset)

    for s in range(1, outer + 2):
        if s < outer:
            each(s, line_blocks)
        if s - 1 < outer:
            each(s - 1, side_blocks)
        if s >= 2:
            each(s - 2, lambda zz, offset: expand_block(zz))
            each(s - 2, lambda zz, offset: scale_block(zz))

    def drain(k, shape):
        ref = cols.at[0] if len(shape) == 2 else rows.at[pl.ds(0, narrow)]
        pltpu.make_async_copy(ref, ref, send_sem.at[k]).wait()

    waits = {}
    for k, (when, shape) in enumerate(pending):
        when = when if isinstance(when, tuple) else (when, None)
        waits.setdefault(when, []).append((k, shape))
    for (offset, kind), items in waits.items():
        test = None
        if offset is not None:
            test = present(offset)
        extra = {"right": z < outer - 1, "left": z > 0, "row": n == holder}.get(kind)
        if extra is not None:
            test = extra if test is None else test & extra

        def all_of(items=items):
            for k, shape in items:
                drain(k, shape)

        if test is None:
            all_of()
        else:
            pl.when(test)(all_of)

    for k in range(count_first(outer, inner * narrow)):
        pltpu.make_async_copy(src, src, first_send.at[k]).wait()


def second_sends(outer, inner, narrow):
    spread = 2 + (inner - 1) + 1
    row = 2 * (narrow - 1)
    sides = (inner - 1) * (narrow + row)
    total = (narrow - 1) * (3 + inner) + spread + narrow - 1 + row + sides
    return total + 2 * (outer - 1) * (narrow * (spread - 1) + row + sides)


def gather_pairs(val, cond, gmap, energies, lists, window, row_window, row_width, tile, wide, narrow):
    num_val, chunk = val.shape
    waves = gmap.shape[1]
    table, codes, line, reach = tables(waves, num_val)
    plane_h, plane_l = np_halves(table)
    line_h, line_l = np_halves(line)
    slots = lists.shape[2]
    outer, inner = wide_factors(wide)
    devices = wide * narrow
    count = codes.shape[0]
    plane = GRID * GRID
    kinds = 2 * reach + 1
    operands = (cond, plane_h, plane_l, line_h, line_l, codes, lists.reshape(1, -1), gmap)
    held = [pltpu.VMEM(x.shape, x.dtype) for x in operands]
    sends = count_first(outer, inner * narrow)
    depth = 2 * num_val
    width = waves // narrow
    num = energies[2].shape[0]
    return pl.pallas_call(
        functools.partial(pairs_kernel, wide, narrow, reach, slots, window, row_window, row_width // 2),
        out_shape=[
            jax.ShapeDtypeStruct((devices * depth, width), jnp.bfloat16),
            jax.ShapeDtypeStruct((num, row_width, devices * depth), jnp.bfloat16),
        ],
        in_specs=[pl.BlockSpec(memory_space=HBM)] * 12,
        out_specs=[pl.BlockSpec(memory_space=VMEM)] * 2,
        scratch_shapes=[pltpu.VMEM((GRID, num_val, plane), jnp.float32)]
        + held
        + [
            pltpu.VMEM((GRID, num_val, 2 * count), jnp.float32),
            pltpu.VMEM((2 * kinds * num_val, count), jnp.bfloat16),
            pltpu.VMEM((count, narrow * slots), jnp.bfloat16),
            pltpu.VMEM((1, narrow * slots), jnp.int32),
            pltpu.VMEM((1, narrow * slots), jnp.float32),
            pltpu.VMEM((narrow - 1, depth, slots), jnp.bfloat16),
            pltpu.VMEM((devices, depth, slots), jnp.bfloat16),
            pltpu.VMEM((devices, depth, row_window), jnp.bfloat16),
            pltpu.VMEM((width // tile, window, tile), jnp.bfloat16),
            pltpu.VMEM((1, width), jnp.float32),
            pltpu.VMEM((row_window, row_width), jnp.bfloat16),
            pltpu.VMEM((1, row_width), jnp.float32),
            pltpu.VMEM((num, devices * depth), jnp.float32),
        ]
        + [pltpu.SMEM(x.shape, x.dtype) for x in energies]
        + [
            pltpu.SemaphoreType.DMA((sends,)),
            pltpu.SemaphoreType.DMA((devices,)),
            pltpu.SemaphoreType.DMA,
            pltpu.SemaphoreType.DMA((11,)),
            pltpu.SemaphoreType.DMA((second_sends(outer, inner, narrow),)),
            pltpu.SemaphoreType.DMA((devices,)),
            pltpu.SemaphoreType.DMA((wide,)),
        ],
        compiler_params=pltpu.CompilerParams(
            collective_id=0, has_side_effects=True, vmem_limit_bytes=24 << 20
        ),
    )(*[pltpu.with_memory_space_constraint(jnp.asarray(x), HBM) for x in (*energies, val, *operands)])


def expansion(listed, index):
    slots, tile = listed.shape[1], index.shape[1]
    area = GRID * GRID
    lx, ly, lz = listed // area, listed // GRID % GRID, listed % GRID
    mirror = (GRID - lx) % GRID * area + (GRID - ly) % GRID * GRID + (GRID - lz) % GRID
    mirror = jnp.where(listed < 0, -1, mirror)

    def column(row):
        turned = jnp.broadcast_to(row, (128, slots)).T
        return jnp.concatenate([turned] * (tile // 128), axis=1)

    hit = (index == column(listed)) | (index == column(mirror))
    kx, ky, kz = index // area, index // GRID % GRID, index % GRID
    low = GRID // 2
    direct = ((kz > 0) & (kz < low)) | (
        (kz == 0) & (((ky > 0) & (ky < low)) | ((ky == 0) & (kx < low)))
    )
    sign = jnp.where(direct, 1.0, -1.0).astype(jnp.float32)
    return jnp.where(hit, 1.0, 0.0).astype(jnp.bfloat16), sign


def chi_kernel(tile, scaled, panel, out, held, sems):
    num, row_width, depth = scaled.shape
    steps = panel.shape[1] // tile

    def copy(slot, i, t):
        here = pl.ds(pl.multiple_of(t * tile, 128), tile)
        return pltpu.make_async_copy(held.at[slot, i], out.at[i, :, here], sems.at[slot, i])

    def product(slot, i, t):
        held[slot, i] = dot(scaled[i], panel[:, pl.ds(pl.multiple_of(t * tile, 128), tile)])

    def body(t, carry):
        slot = lax.rem(t, 2)

        @pl.when(t >= 2)
        def _():
            for i in range(num):
                copy(slot, i, t - 2).wait()

        for i in range(num):
            product(slot, i, t)
        for i in range(num):
            copy(slot, i, t).start()
        return carry

    lax.fori_loop(0, steps - 1, body, 0)
    last = steps - 1
    for i in range(num):
        if last >= 2:
            copy(last % 2, i, last - 2).wait()
        product(last % 2, i, last)
        if i % 2 == 1:
            copy(last % 2, i - 1, last).start()
            copy(last % 2, i, last).start()
    if num % 2:
        copy(last % 2, num - 1, last).start()
    for t in range(max(0, last - 1), steps):
        for i in range(num):
            copy(t % 2, i, t).wait()


def chi_of(scaled, panel, tile):
    num, row_width, depth = scaled.shape
    width = panel.shape[1]
    return pl.pallas_call(
        functools.partial(chi_kernel, tile),
        out_shape=jax.ShapeDtypeStruct((num, row_width, width), jnp.float32),
        in_specs=[pl.BlockSpec(memory_space=VMEM)] * 2,
        out_specs=pl.BlockSpec(memory_space=HBM),
        scratch_shapes=[
            pltpu.VMEM((2, num, row_width, tile), jnp.float32),
            pltpu.SemaphoreType.DMA((2, num)),
        ],
        compiler_params=pltpu.CompilerParams(vmem_limit_bytes=20 << 20),
    )(scaled, panel)


def body(valence, conduction, eps_val, eps_cond, omega, gmap):
    wide, narrow = lax.axis_size("wide"), lax.axis_size("narrow")
    assert conduction.shape[0] == 1
    waves = gmap.shape[0]
    row_width, width = waves // wide, waves // narrow
    tile = min(512, width)
    lists, windows = half_lists(waves, narrow, (row_width, tile))
    band = conduction.reshape(GRID, 1, GRID * GRID)
    energies = (eps_cond, eps_val, omega)
    panel, scaled = gather_pairs(
        valence, band, gmap.reshape(1, waves), energies, lists, windows[tile], windows[row_width],
        row_width, tile, wide, narrow,
    )
    return chi_of(scaled, panel, tile)


def solution(mesh):
    placed = (P(None, ("wide", "narrow")), P(("wide", "narrow"), None), P(), P(), P(), P())
    return jax.shard_map(
        body, mesh=mesh, in_specs=placed, out_specs=P(None, "wide", "narrow"), check_vma=False
    )
```

```python
import functools
import math

import jax
import jax.numpy as jnp
import numpy as np
from jax import lax
from jax.experimental import pallas as pl
from jax.experimental.pallas import tpu as pltpu
from jax.sharding import PartitionSpec as P

GRID = 32
MESH = pl.DeviceIdType.MESH
VMEM = pltpu.MemorySpace.VMEM
HBM = pltpu.MemorySpace.HBM
SMEM = pltpu.MemorySpace.SMEM


def wide_factors(wide):
    chips = wide // 2
    inner = 2 ** (int(math.log2(chips)) // 2)
    return chips // inner, inner


@functools.lru_cache(None)
def tables(num_waves, num_val):
    fold = np.arange(GRID)
    fold = np.where(fold < GRID // 2, fold, fold - GRID)
    squares = fold**2
    lengths = (squares[:, None, None] + squares[None, :, None] + squares[None, None, :]).reshape(-1)
    limit = int(np.sort(lengths)[num_waves - 1])
    reach = math.isqrt(limit)
    assert reach < GRID // 2
    half = [
        (ky, kz)
        for ky in range(-reach, reach + 1)
        for kz in range(0, reach + 1)
        if ky * ky + kz * kz <= limit and (kz > 0 or ky >= 0)
    ]
    count = -(-len(half) // 128) * 128
    kys = np.array([k for k, _ in half])
    kzs = np.array([k for _, k in half])
    points = np.arange(GRID)
    turn = 2.0 * np.pi / GRID
    phase = (points[:, None, None] * kys + points[None, :, None] * kzs) % GRID
    phase = phase.reshape(GRID * GRID, len(half)) * turn
    plane = np.zeros((GRID * GRID, 2 * count))
    plane[:, : len(half)] = np.cos(phase)
    plane[:, count : count + len(half)] = -np.sin(phase)
    codes = np.full((count, 2), -1, np.int32)
    codes[: len(half), 0] = (kys % GRID) * GRID + kzs % GRID
    codes[: len(half), 1] = (-kys % GRID) * GRID + -kzs % GRID
    kxs = np.arange(-reach, reach + 1)
    line = (kxs[:, None] * points[None, :] % GRID) * turn
    eye = np.eye(num_val)
    norm = 1.0 / math.sqrt(GRID**3)
    cosine = np.kron(np.cos(line), eye) * norm
    sine = np.kron(np.sin(line), eye) * norm
    return plane, codes, np.stack([cosine, sine]), reach


def round_up(count, step):
    return -(-count // step) * step


@functools.lru_cache(None)
def half_lists(num_waves, narrow, tiles):
    fold = np.arange(GRID)
    fold = np.where(fold < GRID // 2, fold, fold - GRID)
    kx, ky, kz = [k.reshape(-1) for k in np.meshgrid(fold, fold, fold, indexing="ij")]
    lengths = kx * kx + ky * ky + kz * kz
    ordered = np.sort(lengths)[:num_waves]
    half = (kz > 0) | ((kz == 0) & ((ky > 0) | ((ky == 0) & (kx >= 0))))
    chosen = np.nonzero(half & (lengths <= ordered[-1]))[0]
    chosen = chosen[np.argsort(lengths[chosen], kind="stable")]
    sizes = lengths[chosen]
    part = num_waves // narrow
    ends = []
    for n in range(narrow):
        begin = np.searchsorted(sizes, ordered[n * part])
        ends.append((begin, np.searchsorted(sizes, ordered[(n + 1) * part - 1], side="right")))
    below, above = 0, {tile: 0 for tile in tiles}
    for n, (begin, _) in enumerate(ends):
        for tile in tiles:
            for t in range(part // tile):
                g = n * part + t * tile
                low = np.searchsorted(sizes, ordered[g]) - begin - t * tile // 2
                high = np.searchsorted(sizes, ordered[g + tile - 1], side="right") - begin - t * tile // 2
                below, above[tile] = max(below, -int(low)), max(above[tile], int(high))
    windows = {tile: round_up(below + above[tile], 128) for tile in tiles}
    slots = max((part // tile - 1) * tile // 2 + windows[tile] for tile in tiles)
    slots = max(slots, round_up(below + max(end - begin for begin, end in ends), 128))
    lists = np.full((narrow, 1, slots), -1, np.int32)
    for n, (begin, end) in enumerate(ends):
        lists[n, 0, below : below + end - begin] = chosen[begin:end]
    return lists, windows


def np_halves(table):
    table = np.asarray(table, np.float32)
    high = table.astype(jnp.bfloat16)
    return high, (table - high.astype(np.float32)).astype(jnp.bfloat16)


def split_bf16(x):
    high = x.astype(jnp.bfloat16)
    return high, (x - high.astype(jnp.float32)).astype(jnp.bfloat16)


def dot(a, b):
    return jnp.dot(a, b, preferred_element_type=jnp.float32)


def dot3(a, b_high, b_low):
    a_high, a_low = split_bf16(a)
    return dot(a_high, b_high) + (dot(a_low, b_high) + dot(a_high, b_low))


def dot3_left(a_high, a_low, b):
    b_high, b_low = split_bf16(b)
    return dot(a_high, b_high) + (dot(a_high, b_low) + dot(a_low, b_high))


def flip(i, mask, size):
    assert size & (size - 1) == 0
    out, bit = i, 1
    while bit < size:
        if mask & bit:
            out = out + bit * (1 - 2 * lax.rem(i // bit, 2))
        bit *= 2
    return out


class Place:
    def __init__(self, wide, narrow):
        self.outer, self.inner = wide_factors(wide)
        self.wide, self.narrow = wide, narrow
        self.w, self.n = lax.axis_index("wide"), lax.axis_index("narrow")
        self.core = lax.rem(self.w, 2)
        self.y = lax.rem(self.w // 2, self.inner)
        self.z = self.w // (2 * self.inner)
        self.sizes = dict(z=self.outer, y=self.inner, x=narrow)

    def wide_at(self, zz, yy, cc):
        return (zz * self.inner + yy) * 2 + cc

    def slot(self, zz, yy, cc, nn):
        return self.wide_at(zz, yy, cc) * self.narrow + nn

    def moved(self, masks):
        return (
            flip(self.z, masks.get("z", 0), self.outer),
            flip(self.y, masks.get("y", 0), self.inner),
            flip(self.n, masks.get("x", 0), self.narrow),
        )

    def device(self, masks):
        zz, yy, nn = self.moved(masks)
        return (self.wide_at(zz, yy, self.core), nn)

    def peers(self):
        found = []
        for dim, size in self.sizes.items():
            found += [self.device({dim: m}) for m in range(1, size)]
        other = self.wide_at(self.z, self.y, 1 - self.core)
        found += [(other, flip(self.n, m, self.narrow)) for m in range(self.narrow)]
        for m in range(1, self.narrow):
            for dim in ("y",):
                found += [self.device({dim: k, "x": m}) for k in range(1, self.sizes[dim])]
        return found


def count_first(outer, plane):
    return (outer - 1 + plane) + (outer - 1) * plane + (plane - 1) * outer


def first_gather(place, src, view, send_sem, recv_sem, idle):
    outer, inner, narrow = place.outer, place.inner, place.narrow
    partner = (place.wide_at(place.z, place.y, 1 - place.core), place.n)
    around = [{"y": a, "x": b} for a in range(inner) for b in range(narrow) if a or b]
    around.sort(key=lambda masks: -(masks["y"] > 0) - (masks["x"] > 0))
    count = [0]

    def send(ref, index, target):
        pltpu.make_async_remote_copy(
            src_ref=ref,
            dst_ref=view(index),
            send_sem=send_sem.at[count[0]],
            recv_sem=recv_sem.at[index],
            device_id=target,
            device_id_type=MESH,
        ).start()
        count[0] += 1

    def arrived(index):
        pltpu.make_async_copy(view(index), view(index), recv_sem.at[index]).wait()

    def index_of(masks):
        zz, yy, nn = place.moved(masks)
        return place.slot(zz, yy, place.core, nn)

    mine = index_of({})
    for m in range(outer - 1, 0, -1):
        send(src, mine, place.device({"z": m}))
    for masks in around:
        send(src, mine, place.device(masks))
    send(src, mine, partner)
    idle()
    for m in range(1, outer):
        index = index_of({"z": m})
        arrived(index)
        for masks in around:
            send(view(index), index, place.device(masks))
        send(view(index), index, partner)
    for m in range(outer):
        for masks in around:
            index = index_of({**masks, "z": m})
            arrived(index)
            send(view(index), index, partner)
    assert count[0] == count_first(outer, inner * narrow)


def chunks_of(slots):
    cut = slots // 1024 * 512
    return [(0, cut), (cut, slots - cut)] if cut else [(0, slots)]


def pairs_kernel(wide, narrow, reach, slots, window, row_window, row_step, *refs):
    energies = refs[:3]
    src, sources = refs[3], refs[4:12]
    panel, scaled = refs[12:14]
    val, held = refs[14], refs[15:23]
    stage, picked, pick_hot, pick_x, pick_sign, local = refs[23:29]
    cols, rows, hot, hot_sign, row_hot, row_sign, weights = refs[29:36]
    eps_cond, eps_val, omega = refs[36:39]
    first_send, first_recv, own_sem, load_sem, send_sem, recv_sem, row_recv = refs[39:46]
    cond, plane_h, plane_l, line_h, line_l, codes, lists, gmap = held
    place = Place(wide, narrow)
    core, n, w, z, y = place.core, place.n, place.w, place.z, place.y
    outer, inner = place.outer, place.inner
    grid, num_val, plane = val.shape
    devices = wide * narrow
    chunk = src.shape[1]
    per = plane // chunk
    count = codes.shape[0]
    kinds = 2 * reach + 1
    size = kinds * num_val
    chunks = chunks_of(slots)

    copies = [pltpu.make_async_copy(a, b, load_sem.at[i]) for i, (a, b) in enumerate(zip([*sources, *energies], [*held, eps_cond, eps_val, omega]))]
    for i in (5, 6, 0, 1, 2, 3, 4, 7, 8, 9, 10):
        copies[i].start()

    peers = place.peers()
    barrier = pltpu.get_barrier_semaphore()
    for peer in peers:
        pl.semaphore_signal(barrier, inc=1, device_id=peer, device_id_type=MESH)
    pl.semaphore_wait(barrier, len(peers))

    def view(index):
        if per == 1:
            return val.at[index]
        return val.at[index // per, :, pl.ds(pl.multiple_of(lax.rem(index, per) * chunk, chunk), chunk)]

    mine = place.slot(z, y, core, n)
    own = pltpu.make_async_copy(src, view(mine), own_sem)
    own.start()

    def prepare():
        copies[5].wait()
        copies[6].wait()
        first, second = codes[:, 0:1], codes[:, 1:2]
        tile = 256 if pick_hot.shape[1] % 256 == 0 else 128

        def body(t, carry):
            here = pl.ds(pl.multiple_of(t * tile, tile), tile)
            index = jnp.maximum(lists[:, here], 0)
            kx = index // (GRID * GRID)
            code = index % (GRID * GRID)
            ky, kz = code // GRID, code % GRID
            kx = jnp.where(kx < GRID // 2, kx, kx - GRID)
            direct = ((kz > 0) & (kz < GRID // 2)) | ((kz == 0) & (ky < GRID // 2))
            pick_x[:, here] = jnp.where(direct, kx, -kx) + reach
            pick_sign[:, here] = jnp.where(direct, 1.0, -1.0).astype(jnp.float32)
            hit = (code == first) | (code == second)
            pick_hot[:, here] = jnp.where(hit, 1.0, 0.0).astype(jnp.bfloat16)
            return carry

        lax.fori_loop(0, pick_hot.shape[1] // tile, body, 0)

    first_gather(place, src, view, first_send, first_recv, prepare)

    own.wait()
    step = narrow // per

    def flat(cc):
        copies_of = [(2 * q + cc) * step for q in range(wide // 2)]
        field = [(val[pl.ds(p, step)] * cond[pl.ds(p, step)]).reshape(step * num_val, plane) for p in copies_of]
        result = dot3(jnp.concatenate(field, axis=0), plane_h[...], plane_l[...])
        for q, p in enumerate(copies_of):
            part = result[q * step * num_val : (q + 1) * step * num_val]
            stage[pl.ds(p, step)] = part.reshape(step, num_val, 2 * count)

    for i in range(3):
        copies[i].wait()
    flat(core)
    for zz in range(outer):
        for yy in range(inner):
            for nn in range(narrow):
                index = place.slot(zz, yy, 1 - core, nn)
                pltpu.make_async_copy(view(index), view(index), first_recv.at[index]).wait()
    flat(1 - core)
    copies[3].wait()
    copies[4].wait()
    whole = stage[...].reshape(grid * num_val, 2 * count)
    real, imag = whole[:, :count], whole[:, count:]
    cos_h, sin_h, cos_l, sin_l = line_h[0], line_h[1], line_l[0], line_l[1]
    picked[:size, :] = (dot3_left(cos_h, cos_l, real) + dot3_left(sin_h, sin_l, imag)).astype(jnp.bfloat16)
    picked[size:, :] = (dot3_left(cos_h, cos_l, imag) - dot3_left(sin_h, sin_l, real)).astype(jnp.bfloat16)

    def pick(half, store, ready):
        base = pl.multiple_of(half * slots, 128)
        for begin in range(0, slots, 512):
            tile = min(512, slots - begin)
            here = pl.ds(pl.multiple_of(base + begin, 128), tile)
            columns = dot(picked[...], pick_hot[:, here]).reshape(2, kinds, num_val, tile)
            kx = jnp.broadcast_to(pick_x[:, here], (num_val, tile))
            sign = pick_sign[:, here]
            real = jnp.zeros((num_val, tile), jnp.float32)
            imag = jnp.zeros((num_val, tile), jnp.float32)
            for k in range(kinds):
                keep = kx == k
                real = jnp.where(keep, columns[0, k], real)
                imag = jnp.where(keep, columns[1, k], imag)
            store(begin, tile, jnp.concatenate([real, imag * sign], axis=0).astype(jnp.bfloat16))
            for number, (start, length) in enumerate(chunks):
                if begin + tile == start + length:
                    ready(number)

    partner = (place.wide_at(z, y, 1 - core), n)
    pending = []

    def send(src_ref, dst_ref, target, sem, when=None):
        k = len(pending)
        pltpu.make_async_remote_copy(
            src_ref=src_ref,
            dst_ref=dst_ref,
            send_sem=send_sem.at[k],
            recv_sem=sem,
            device_id=target,
            device_id_type=MESH,
        ).start()
        pending.append((when, src_ref.shape))

    def part(ref, number):
        return ref.at[:, pl.ds(*chunks[number])]

    def forward(index, number, target, when=None):
        ref = part(cols.at[index], number)
        send(ref, ref, target, recv_sem.at[index, number], when)

    def arrived(index, number):
        ref = part(cols.at[index], number)
        pltpu.make_async_copy(ref, ref, recv_sem.at[index, number]).wait()

    holder = w // (wide // narrow)
    window_of = lambda ww: pl.multiple_of(lax.rem(ww, wide // narrow) * row_step, 128)
    others = [m for m in range(1, narrow)]

    def row_sends(zz, yy, when):
        start = place.slot(zz, yy, core, 0)
        group = (zz * inner + yy) * 2 + core

        @pl.when(n == holder)
        def _():
            for cc in (core, 1 - core):
                ww = place.wide_at(z, y, cc)
                for m in others:
                    send(
                        cols.at[pl.ds(start, narrow), :, pl.ds(window_of(ww), row_window)],
                        rows.at[pl.ds(start, narrow)],
                        (ww, flip(n, m, narrow)),
                        row_recv.at[group],
                        (when, "row"),
                    )

    block = devices // outer
    block_rows = block * 2 * num_val
    tile = hot.shape[2]

    def prepare_hot():
        for copy in copies[7:]:
            copy.wait()
        num_cond, num = eps_cond.shape[0], omega.shape[0]
        depth = panel.shape[0]
        lane = lax.broadcasted_iota(jnp.int32, (1, depth), 1)
        band, orbital = lane // (2 * num_val), lane % num_val

        def choose(ref, where):
            def select(i, held):
                return jnp.where(where == i, ref[i], held)

            return lax.fori_loop(0, ref.shape[0], select, jnp.zeros((1, depth), jnp.float32))

        gap = choose(eps_cond, band) - choose(eps_val, orbital)
        norm = math.sqrt(num_cond * num_val)
        for i in range(num):
            weights[i : i + 1, :] = -2.0 * gap / (gap * gap + omega[i] * omega[i]) / norm

        row_width = row_hot.shape[1]
        first = pl.multiple_of(holder * slots + lax.rem(w, wide // narrow) * row_step, 128)
        index = gmap[:, pl.ds(pl.multiple_of(w * row_width, 128), row_width)]
        row_hot[...], row_sign[...] = expansion(lists[:, pl.ds(first, row_window)], index)

        def body(t, carry):
            first = pl.multiple_of(n * slots + t * (tile // 2), 128)
            here = pl.ds(pl.multiple_of(t * tile, 128), tile)
            index = gmap[:, pl.ds(pl.multiple_of(n * (tile * hot.shape[0]) + t * tile, 128), tile)]
            hot[t], hot_sign[:, here] = expansion(lists[:, pl.ds(first, window)], index)
            return carry

        lax.fori_loop(0, hot.shape[0], body, 0)

    def signed(values, sign):
        row = lax.broadcasted_iota(jnp.int32, values.shape, 0)
        return values * jnp.where(row // num_val % 2 == 1, sign, 1.0)

    def expand_block(zz):
        first = zz * block
        base = pl.multiple_of(zz * block_rows, 16)
        for yy in range(inner):
            for nn in range(narrow):
                for number in range(len(chunks)):
                    arrived(place.slot(zz, yy, 1 - core, nn), number)

        def body(t, carry):
            source = cols[pl.ds(first, block), :, pl.ds(pl.multiple_of(t * (tile // 2), 128), window)]
            here = pl.ds(pl.multiple_of(t * tile, 128), tile)
            values = dot(source.reshape(block_rows, window), hot[t])
            panel[pl.ds(base, block_rows), here] = signed(values, hot_sign[:, here]).astype(jnp.bfloat16)
            return carry

        lax.fori_loop(0, hot.shape[0], body, 0, unroll=4)

    def scale_block(zz):
        first = zz * block
        here = pl.ds(pl.multiple_of(zz * block_rows, 128), block_rows)

        @pl.when(n == holder)
        def _():
            rows[pl.ds(first, block)] = cols[pl.ds(first, block), :, pl.ds(window_of(w), row_window)]

        @pl.when(n != holder)
        def _():
            for group in range(block // narrow):
                rows_of = rows.at[pl.ds(first + group * narrow, narrow)]
                pltpu.make_async_copy(rows_of, rows_of, row_recv.at[zz * (block // narrow) + group]).wait()

        values = dot(rows[pl.ds(first, block)].reshape(block_rows, row_window), row_hot[...])
        turned = signed(values, row_sign[...]).T
        for i in range(scaled.shape[0]):
            scaled[i, :, here] = (turned * weights[i : i + 1, here]).astype(jnp.bfloat16)

    for m in range(narrow - 1, 0, -1):
        half = flip(n, m, narrow)

        def store(begin, tile, value, m=m):
            local[m - 1, :, begin : begin + tile] = value

        def ready(number, m=m, half=half):
            piece, there = part(local.at[m - 1], number), part(cols.at[mine], number)
            sem = recv_sem.at[mine, number]
            send(piece, there, (w, half), sem)

        pick(half, store, ready)

    def store_own(begin, tile, value):
        cols[mine, :, begin : begin + tile] = value

    right, left = (place.wide_at(z + 1, y, core), n), (place.wide_at(z - 1, y, core), n)

    def spread(index, number, when, go_right, go_left):
        if go_right:
            @pl.when(z < outer - 1)
            def _():
                forward(index, number, right, (when, "right"))
        if go_left:
            @pl.when(z > 0)
            def _():
                forward(index, number, left, (when, "left"))
        for m in range(1, inner):
            forward(index, number, place.device({"y": m}), (when, None))
        forward(index, number, partner, (when, None))

    pick(n, store_own, lambda number: spread(mine, number, None, True, True))
    prepare_hot()
    for m in others:
        index = place.slot(z, y, core, flip(n, m, narrow))
        for number in range(len(chunks)):
            arrived(index, number)
            spread(index, number, None, True, True)
    row_sends(z, y, None)

    def side_blocks(zz, when):
        for m in range(1, inner):
            yy = flip(y, m, inner)
            for k in range(narrow):
                index = place.slot(zz, yy, core, flip(n, k, narrow))
                for number in range(len(chunks)):
                    arrived(index, number)
                    forward(index, number, partner, (when, None))
            row_sends(zz, yy, when)

    def present(offset):
        return (z + offset >= 0) & (z + offset < outer)

    def each(s, work):
        if s == 0:
            work(z, None)
            return
        for offset in (-s, s):
            @pl.when(present(offset))
            def _():
                work(z + offset, offset)

    def line_blocks(zz, offset):
        for k in range(narrow):
            index = place.slot(zz, y, core, flip(n, k, narrow))
            for number in range(len(chunks)):
                arrived(index, number)
                spread(index, number, offset, offset < 0, offset > 0)
        row_sends(zz, y, offset)

    for s in range(1, outer + 2):
        if s < outer:
            each(s, line_blocks)
        if s - 1 < outer:
            each(s - 1, side_blocks)
        if s >= 2:
            each(s - 2, lambda zz, offset: expand_block(zz))
            each(s - 2, lambda zz, offset: scale_block(zz))

    def drain(k, shape):
        ref = cols.at[0, :, pl.ds(0, shape[1])] if len(shape) == 2 else rows.at[pl.ds(0, narrow)]
        pltpu.make_async_copy(ref, ref, send_sem.at[k]).wait()

    assert len(pending) == send_sem.shape[0]
    waits = {}
    for k, (when, shape) in enumerate(pending):
        when = when if isinstance(when, tuple) else (when, None)
        waits.setdefault(when, []).append((k, shape))
    for (offset, kind), items in waits.items():
        test = None
        if offset is not None:
            test = present(offset)
        extra = {"right": z < outer - 1, "left": z > 0, "row": n == holder}.get(kind)
        if extra is not None:
            test = extra if test is None else test & extra

        def all_of(items=items):
            for k, shape in items:
                drain(k, shape)

        if test is None:
            all_of()
        else:
            pl.when(test)(all_of)

    for k in range(count_first(outer, inner * narrow)):
        pltpu.make_async_copy(src, src, first_send.at[k]).wait()


def second_sends(outer, inner, narrow, chunks):
    near = 2 * (outer - 1)
    pieces = (narrow - 1) * 1 + narrow * (inner + 2) + 0 * inner
    pieces += near * narrow * (inner + 1) + (near + 1) * (inner - 1) * narrow
    return pieces * chunks + (near + 1) * inner * 2 * (narrow - 1)


def gather_pairs(val, cond, gmap, energies, lists, window, row_window, row_width, tile, wide, narrow):
    num_val, chunk = val.shape
    waves = gmap.shape[1]
    table, codes, line, reach = tables(waves, num_val)
    plane_h, plane_l = np_halves(table)
    line_h, line_l = np_halves(line)
    slots = lists.shape[2]
    outer, inner = wide_factors(wide)
    devices = wide * narrow
    count = codes.shape[0]
    plane = GRID * GRID
    kinds = 2 * reach + 1
    operands = (cond, plane_h, plane_l, line_h, line_l, codes, lists.reshape(1, -1), gmap)
    held = [pltpu.VMEM(x.shape, x.dtype) for x in operands]
    sends = count_first(outer, inner * narrow)
    depth = 2 * num_val
    width = waves // narrow
    num = energies[2].shape[0]
    return pl.pallas_call(
        functools.partial(pairs_kernel, wide, narrow, reach, slots, window, row_window, row_width // 2),
        out_shape=[
            jax.ShapeDtypeStruct((devices * depth, width), jnp.bfloat16),
            jax.ShapeDtypeStruct((num, row_width, devices * depth), jnp.bfloat16),
        ],
        in_specs=[pl.BlockSpec(memory_space=HBM)] * 12,
        out_specs=[pl.BlockSpec(memory_space=VMEM)] * 2,
        scratch_shapes=[pltpu.VMEM((GRID, num_val, plane), jnp.float32)]
        + held
        + [
            pltpu.VMEM((GRID, num_val, 2 * count), jnp.float32),
            pltpu.VMEM((2 * kinds * num_val, count), jnp.bfloat16),
            pltpu.VMEM((count, narrow * slots), jnp.bfloat16),
            pltpu.VMEM((1, narrow * slots), jnp.int32),
            pltpu.VMEM((1, narrow * slots), jnp.float32),
            pltpu.VMEM((narrow - 1, depth, slots), jnp.bfloat16),
            pltpu.VMEM((devices, depth, slots), jnp.bfloat16),
            pltpu.VMEM((devices, depth, row_window), jnp.bfloat16),
            pltpu.VMEM((width // tile, window, tile), jnp.bfloat16),
            pltpu.VMEM((1, width), jnp.float32),
            pltpu.VMEM((row_window, row_width), jnp.bfloat16),
            pltpu.VMEM((1, row_width), jnp.float32),
            pltpu.VMEM((num, devices * depth), jnp.float32),
        ]
        + [pltpu.SMEM(x.shape, x.dtype) for x in energies]
        + [
            pltpu.SemaphoreType.DMA((sends,)),
            pltpu.SemaphoreType.DMA((devices,)),
            pltpu.SemaphoreType.DMA,
            pltpu.SemaphoreType.DMA((11,)),
            pltpu.SemaphoreType.DMA((second_sends(outer, inner, narrow, len(chunks_of(slots))),)),
            pltpu.SemaphoreType.DMA((devices, len(chunks_of(slots)))),
            pltpu.SemaphoreType.DMA((wide,)),
        ],
        compiler_params=pltpu.CompilerParams(
            collective_id=0, has_side_effects=True, vmem_limit_bytes=24 << 20
        ),
    )(*[pltpu.with_memory_space_constraint(jnp.asarray(x), HBM) for x in (*energies, val, *operands)])


def expansion(listed, index):
    slots, tile = listed.shape[1], index.shape[1]
    area = GRID * GRID
    lx, ly, lz = listed // area, listed // GRID % GRID, listed % GRID
    mirror = (GRID - lx) % GRID * area + (GRID - ly) % GRID * GRID + (GRID - lz) % GRID
    mirror = jnp.where(listed < 0, -1, mirror)

    def column(row):
        turned = jnp.broadcast_to(row, (128, slots)).T
        return jnp.concatenate([turned] * (tile // 128), axis=1)

    hit = (index == column(listed)) | (index == column(mirror))
    kx, ky, kz = index // area, index // GRID % GRID, index % GRID
    low = GRID // 2
    direct = ((kz > 0) & (kz < low)) | (
        (kz == 0) & (((ky > 0) & (ky < low)) | ((ky == 0) & (kx < low)))
    )
    sign = jnp.where(direct, 1.0, -1.0).astype(jnp.float32)
    return jnp.where(hit, 1.0, 0.0).astype(jnp.bfloat16), sign


def chi_kernel(tile, scaled, panel, out, held, sems):
    num, row_width, depth = scaled.shape
    steps = panel.shape[1] // tile

    def copy(slot, i, t):
        here = pl.ds(pl.multiple_of(t * tile, 128), tile)
        return pltpu.make_async_copy(held.at[slot, i], out.at[i, :, here], sems.at[slot, i])

    def product(slot, i, t):
        held[slot, i] = dot(scaled[i], panel[:, pl.ds(pl.multiple_of(t * tile, 128), tile)])

    def body(t, carry):
        slot = lax.rem(t, 2)

        @pl.when(t >= 2)
        def _():
            for i in range(num):
                copy(slot, i, t - 2).wait()

        for i in range(num):
            product(slot, i, t)
        for i in range(num):
            copy(slot, i, t).start()
        return carry

    lax.fori_loop(0, steps - 1, body, 0)
    last = steps - 1
    for i in range(num):
        if last >= 2:
            copy(last % 2, i, last - 2).wait()
        product(last % 2, i, last)
        if i % 2 == 1:
            copy(last % 2, i - 1, last).start()
            copy(last % 2, i, last).start()
    if num % 2:
        copy(last % 2, num - 1, last).start()
    for t in range(max(0, last - 1), steps):
        for i in range(num):
            copy(t % 2, i, t).wait()


def chi_of(scaled, panel, tile):
    num, row_width, depth = scaled.shape
    width = panel.shape[1]
    return pl.pallas_call(
        functools.partial(chi_kernel, tile),
        out_shape=jax.ShapeDtypeStruct((num, row_width, width), jnp.float32),
        in_specs=[pl.BlockSpec(memory_space=VMEM)] * 2,
        out_specs=pl.BlockSpec(memory_space=HBM),
        scratch_shapes=[
            pltpu.VMEM((2, num, row_width, tile), jnp.float32),
            pltpu.SemaphoreType.DMA((2, num)),
        ],
        compiler_params=pltpu.CompilerParams(vmem_limit_bytes=20 << 20),
    )(scaled, panel)


def body(valence, conduction, eps_val, eps_cond, omega, gmap):
    wide, narrow = lax.axis_size("wide"), lax.axis_size("narrow")
    assert conduction.shape[0] == 1
    waves = gmap.shape[0]
    row_width, width = waves // wide, waves // narrow
    tile = min(512, width)
    lists, windows = half_lists(waves, narrow, (row_width, tile))
    band = conduction.reshape(GRID, 1, GRID * GRID)
    energies = (eps_cond, eps_val, omega)
    panel, scaled = gather_pairs(
        valence, band, gmap.reshape(1, waves), energies, lists, windows[tile], windows[row_width],
        row_width, tile, wide, narrow,
    )
    return chi_of(scaled, panel, tile)


def solution(mesh):
    placed = (P(None, ("wide", "narrow")), P(("wide", "narrow"), None), P(), P(), P(), P())
    return jax.shard_map(
        body, mesh=mesh, in_specs=placed, out_specs=P(None, "wide", "narrow"), check_vma=False
    )
```
